128 devices in a mesh: rows: 128 (over x, y, z, core).
Axes of the slice: x: 4, y: 4, z: 4, core: 2. Of those that a mesh axis runs over, the one named last changes fastest.
Arguments:
- right_side: float32 [9, 16384], P(None, 'rows'), may hold values from -30 to 30
- diag_blocks: float32 [9, 9, 16384], P(None, None, 'rows'), may hold values from -40 to 45, as said below
- precond: float32 [9, 9, 16384], P(None, None, 'rows'), may hold values from -5 to 5, as said below
- upper_blocks: float32 [8, 9, 9, 16384], P(None, None, None, 'rows'), may hold values from -0.21875 to 0.21875
- block_cols: int32 [8, 16384], P(None, 'rows'), may hold values from 0 to 16383, as said below
- slot_of_camera: int32 [16384], replicated, may hold values from 0 to 16383, as said below
Outputs:
- solution: float32 [9, 16384], P(None, 'rows')
- residual: float32 [9, 16384], P(None, 'rows')
The draws below stay inside these ranges and needn't reach their ends.
Inputs may be any that keep to these rules, and one draw needn't show every extreme that they name: slot_of_camera is a permutation; slot s is held by the device s // 128. `block_cols`: for every device d and every device e, exactly 8 of the entries of the lists of the rows held by d name cameras whose slot is held by e. A list may name a camera more than once, or the row's own camera; every entry adds its block. `diag_blocks`: each 9 x 9 block over the first two dimensions is symmetric positive definite. `precond`: each 9 x 9 block over the first two dimensions is symmetric positive definite.
All inputs are finite; a program needn't handle non-finite values.
Results may differ from the reference program's by a relative error of at most 0.0001.
Values sent between devices are 32-bit elements; how exact they have to be, the bound alone decides.
A program may use at most 64 MiB of HBM per device.

```python
import math
import jax
import jax.numpy as jnp
from jax import lax

BLOCK = 9
NB = 8
CAM_DEV = 128
ITERS = 2
CAMERAS = 16384
REFS = 8
N_ROWS = 128


def camera_graph(key):
    base = jax.random.fold_in(key, 11)
    key_home, key_pick, key_order = jax.random.split(base, 3)
    slot_map = jax.random.permutation(key_home, CAMERAS).astype(jnp.int32)
    camera_at_slot = jnp.argsort(slot_map).astype(jnp.int32)
    chosen = jax.random.randint(key_pick, (N_ROWS, N_ROWS, REFS), 0, CAM_DEV)
    targets = chosen + (jnp.arange(N_ROWS, dtype=jnp.int32) * CAM_DEV)[None, :, None]
    targets = targets.reshape(N_ROWS, CAM_DEV * NB)
    shuffles = jax.vmap(lambda subkey: jax.random.permutation(subkey, CAM_DEV * NB))(jax.random.split(key_order, N_ROWS))
    placed = jnp.take_along_axis(targets, shuffles, axis=1).reshape(N_ROWS, NB, CAM_DEV)
    slot_lists = jnp.transpose(placed, (1, 0, 2)).reshape(NB, CAMERAS)
    return (slot_map, camera_at_slot[slot_lists].astype(jnp.int32))


def draw_slot_of_camera(key, part):
    return camera_graph(key)[0]


def draw_block_cols(key, part):
    return camera_graph(key)[1]


def spd_blocks(key, lift, low, high):
    key_factor, key_scale = jax.random.split(key)
    factor = jnp.clip(jax.random.normal(key_factor, (BLOCK, BLOCK, CAMERAS), jnp.float32), -3.0, 3.0)
    blocks = jnp.einsum('ikc,jkc->ijc', factor, factor) / BLOCK + lift * jnp.eye(BLOCK, dtype=jnp.float32)[:, :, None]
    scales = jnp.exp(jax.random.uniform(key_scale, (CAMERAS,), jnp.float32, math.log(low), math.log(high)))
    return blocks * scales[None, None, :]


def draw_diag_blocks(key, part):
    return spd_blocks(jax.random.fold_in(key, 21), 1.5, 1.0, 4.0)


def draw_precond(key, part):
    return spd_blocks(jax.random.fold_in(key, 22), 0.5, 0.1, 0.5)


def draw_right_side(key, part):
    key_value, key_scale = jax.random.split(jax.random.fold_in(key, 31))
    position = jnp.arange(CAMERAS, dtype=jnp.float32) / max(CAMERAS - 1, 1)
    rough = jnp.exp(jax.random.uniform(key_scale, (CAMERAS,), jnp.float32, math.log(0.6), math.log(6.0)))
    scales = (1.0 + 2.0 * position) / 3.0 * rough
    values = jnp.clip(jax.random.normal(key_value, (BLOCK, CAMERAS), jnp.float32), -4.0, 4.0)
    return values * scales[None, :]


def block_levels(own_key, extent, cuts, smallest, high):
    def one(axis_at, shards_of):
        heights = jax.random.uniform(jax.random.fold_in(jax.random.fold_in(own_key, 6), axis_at), (shards_of,), jnp.float32, smallest / len(cuts), high / len(cuts))
        return jnp.repeat(jnp.exp(heights), extent[axis_at] // shards_of).reshape((-1,) + (1,) * (len(extent) - axis_at - 1))

    gain = one(*cuts[0])
    for cut in cuts[1:]:
        gain = gain * one(*cut)
    return gain


def centred(rng, extent, scale, reach, shards=(), kind=jnp.bfloat16):
    values = scale * jax.random.normal(rng, extent, jnp.float32)
    if shards:
        values = values * block_levels(rng, extent, shards, -0.22, 0.18)
    return jnp.clip(values, -reach, reach).astype(kind)


def setup_inputs(seed: int = 0) -> dict:
    keys = jax.random.split(jax.random.key(seed), 7)
    return {
        "right_side": draw_right_side(jax.random.fold_in(keys[6], 71), 0),
        "diag_blocks": draw_diag_blocks(jax.random.fold_in(keys[6], 71), 0),
        "precond": draw_precond(jax.random.fold_in(keys[6], 71), 0),
        "upper_blocks": centred(keys[3], (NB, BLOCK, BLOCK, CAMERAS), (96 * NB) ** -0.5, 0.21875, ((3, 128),), jnp.float32),
        "block_cols": draw_block_cols(jax.random.fold_in(keys[6], 71), 0),
        "slot_of_camera": draw_slot_of_camera(jax.random.fold_in(keys[6], 71), 0),
    }


def apply_system(operand, diag_blocks, upper_blocks, slot_lists):
    highest = lax.Precision.HIGHEST
    result = jnp.einsum('abc,bc->ac', diag_blocks, operand, precision=highest)
    gathered = operand[:, slot_lists]
    result = result + jnp.einsum('kabc,bkc->ac', upper_blocks, gathered, precision=highest)
    spread = jnp.einsum('kabc,ac->bkc', upper_blocks, operand, precision=highest)
    result = result.at[:, slot_lists.reshape(-1)].add(spread.reshape(BLOCK, -1))
    return result


def reference(right_side, diag_blocks, precond, upper_blocks, block_cols, slot_of_camera):
    highest = lax.Precision.HIGHEST
    slot_lists = slot_of_camera[block_cols].astype(jnp.int32)
    solution = jnp.zeros_like(right_side)
    residual = right_side
    precond_res = jnp.einsum('abc,bc->ac', precond, residual, precision=highest)
    direction = precond_res
    res_dot = jnp.sum(residual * precond_res)
    for step in range(ITERS):
        image = apply_system(direction, diag_blocks, upper_blocks, slot_lists)
        step_size = res_dot / jnp.sum(direction * image)
        solution = solution + step_size * direction
        residual = residual - step_size * image
        if step + 1 < ITERS:
            precond_res = jnp.einsum('abc,bc->ac', precond, residual, precision=highest)
            new_dot = jnp.sum(residual * precond_res)
            direction = precond_res + (new_dot / res_dot) * direction
            res_dot = new_dot
    return solution, residual
```

```python
import functools
import itertools

import jax
import jax.numpy as jnp
from jax import lax
from jax.experimental import pallas as pl
from jax.experimental.pallas import tpu as pltpu
from jax.sharding import PartitionSpec as P

MESH = pl.DeviceIdType.MESH
B = 9
K = 8
N = 128
F32, BF16, I32 = jnp.float32, jnp.bfloat16, jnp.int32


def hops(d):
    return sum(min(k, 4 - k) for k in d[:3])


STEPS = sorted(
    (d for d in itertools.product(range(4), range(4), range(4), range(2)) if any(d)),
    key=lambda d: -hops(d),
)


def targets(me):
    x, y, z, c = me // 32, lax.rem(me // 8, 4), lax.rem(me // 2, 4), lax.rem(me, 2)
    tx = [lax.rem(x + d, 4) * 32 for d in range(4)]
    ty = [lax.rem(y + d, 4) * 8 for d in range(4)]
    tz = [lax.rem(z + d, 4) * 2 for d in range(4)]
    tc = [c, 1 - c]
    xy = {(i, j): tx[i] + ty[j] for i in range(4) for j in range(4)}
    zc = {(i, j): tz[i] + tc[j] for i in range(4) for j in range(2)}
    return [xy[d[0], d[1]] + zc[d[2], d[3]] for d in STEPS]


def iota(shape, dim):
    return lax.broadcasted_iota(I32, shape, dim)


def lanes(x, idx):
    return jnp.take_along_axis(x, idx, axis=1, mode="promise_in_bounds")


def rows8(row):
    return jnp.broadcast_to(row, (K, N))


def pieces(x):
    hi = x.astype(BF16)
    rest = x - hi.astype(F32)
    mid = rest.astype(BF16)
    return hi, mid, (rest - mid.astype(F32)).astype(BF16)


def dot_t(a, b):
    return lax.dot_general(a, b, (((1,), (1,)), ((), ())), preferred_element_type=F32)


def blocks_times(m_ref, v):
    total = m_ref[0] * v[0:1]
    for a in range(1, B):
        total = total + m_ref[a] * v[a : a + 1]
    return total


def kernel(
    b_hbm, d_hbm, p_hbm, u_hbm, c_hbm, t_hbm, x_ref, r_ref,
    b_v, d_v, p_v, u_v, c_v, t_v, in_sem,
    s0, m0, s1, m1, s2, m2, s3, m3, send, recv, pt, ft,
):
    me = lax.axis_index("rows")
    peers = targets(me)
    barrier = pltpu.get_barrier_semaphore()
    for t in peers:
        pl.semaphore_signal(barrier, inc=1, device_id=(t,), device_id_type=MESH)
    copies = [
        pltpu.make_async_copy(src, dst, in_sem.at[i])
        for i, (src, dst) in enumerate(
            [(c_hbm, c_v), (t_hbm, t_v), (b_hbm, b_v), (p_hbm, p_v), (u_hbm, u_v), (d_hbm, d_v)]
        )
    ]
    for c in copies:
        c.start()

    def exchange(n, src, dst, one=False):
        for t in peers:
            pltpu.make_async_remote_copy(
                src_ref=src.at[0 if one else t],
                dst_ref=dst.at[me],
                send_sem=send.at[n],
                recv_sem=recv.at[n],
                device_id=(t,),
                device_id_type=MESH,
            ).start()
        dst[me] = src[0] if one else src[me]

    def arrived(n, dst):
        pltpu.make_async_copy(dst.at[0 : N - 1], dst.at[0 : N - 1], recv.at[n]).wait()

    copies[0].wait()
    copies[1].wait()
    cams = c_v[...]
    hi, lo = cams >> 7, cams & 127
    slots = jnp.zeros((K, N), I32)
    for r in range(N):
        slots = jnp.where(hi == r, lanes(rows8(t_v[r : r + 1, :]), lo), slots)
    owner, offset = slots >> 7, slots & 127

    sub = iota((N, N), 0)
    picks = [sub == owner[k : k + 1, :] for k in range(K)]
    ones = [jnp.where(p, 1.0, 0.0).astype(BF16) for p in picks]
    by_owner = jnp.concatenate(ones, axis=1)
    before = jnp.where(sub < iota((N, N), 1), 1.0, 0.0).astype(BF16)
    stacked = jnp.concatenate(ones, axis=0)
    earlier = jnp.dot(stacked, before, preferred_element_type=F32)
    counts = jnp.dot(stacked, jnp.ones((N, N), BF16), preferred_element_type=F32)
    base = jnp.zeros((N, N), F32)
    ranks = []
    for k in range(K):
        here = earlier[k * N : (k + 1) * N] + base
        ranks.append(jnp.sum(jnp.where(picks[k], here, 0.0), axis=0, keepdims=True))
        base = base + counts[k * N : (k + 1) * N]
    rank = jnp.concatenate(ranks, axis=0).astype(I32)
    sub8 = iota((K, N), 0)
    places = [rank[k : k + 1, :] == sub8 for k in range(K)]

    def spread(v):
        out = []
        for b in range(B):
            total = u_v[0, b] * v[0:1]
            for a in range(1, B):
                total = total + u_v[a, b] * v[a : a + 1]
            out.append(total)
        return out

    def to_owners(lists):
        wide = jnp.concatenate(
            [
                jnp.concatenate(
                    [jnp.where(places[k], rows8(e[k : k + 1, :]), 0.0) for k in range(K)], axis=1
                )
                for e in lists
            ]
            + [jnp.zeros((N - K * len(lists), K * N), F32)],
            axis=0,
        )
        h, m, l = pieces(wide)
        return dot_t(by_owner, h) + dot_t(by_owner, m) + dot_t(by_owner, l)

    def answers(v, asked):
        parts = [lanes(rows8(v[b : b + 1]), asked) for b in range(B)]
        return jnp.concatenate(parts + [jnp.zeros((N - K * B, N), F32)], axis=0).T

    def scatter(got, onehot):
        pt[...] = got[0 : K * B]
        flat = jnp.concatenate([pt[pl.ds(r, B, stride=K), :] for r in range(K)], axis=1)
        h, m, l = pieces(flat)
        return dot_t(h, onehot) + dot_t(m, onehot) + dot_t(l, onehot)

    def forward(got):
        ft[...] = got[0 : K * B]
        total = [jnp.zeros((K, N), F32) for _ in range(B)]
        for b in range(B):
            g = jnp.zeros((K, N), F32)
            for r in range(K):
                row = rows8(ft[K * b + r : K * b + r + 1, :])
                g = jnp.where(rank == r, lanes(row, owner), g)
            for a in range(B):
                total[a] = total[a] + u_v[a, b] * g
        return jnp.concatenate([jnp.sum(t, axis=0, keepdims=True) for t in total], axis=0)

    copies[2].wait()
    copies[3].wait()
    rhs = b_v[...]
    z0 = blocks_times(p_v, rhs)
    copies[4].wait()
    copies[5].wait()
    s0[:, 0, :] = to_owners(spread(z0) + [offset.astype(F32)])
    pl.semaphore_wait(barrier, N - 1)
    exchange(0, s0, m0)

    lane = iota((N, N), 1)
    partial = blocks_times(d_v, z0)
    rho0_part = jnp.sum(rhs * z0)
    arrived(0, m0)
    got = m0[:, 0, :].T
    asked = got[K * B : K * B + K].astype(I32)
    s1[:, 0, :] = answers(z0, asked)
    exchange(1, s1, m1)
    onehot = jnp.concatenate(
        [jnp.where(sub == asked[r : r + 1, :], 1.0, 0.0).astype(BF16) for r in range(K)], axis=1
    )
    partial = partial + scatter(got, onehot)
    arrived(1, m1)
    q0 = partial + forward(m1[:, 0, :].T)

    w0 = blocks_times(p_v, q0)
    c0_part = jnp.sum(z0 * q0)
    out = to_owners(spread(w0))
    s2[:, 0, :] = jnp.where(lane == 80, rho0_part, jnp.where(lane == 81, c0_part, out))
    s2[:, 1, :] = answers(w0, asked)
    exchange(2, s2, m2)
    partial = blocks_times(d_v, w0)
    arrived(2, m2)
    first = m2[:, 0, :]
    sums = jnp.sum(first, axis=0, keepdims=True)
    lane1 = iota((1, N), 1)
    rho0 = jnp.sum(jnp.where(lane1 == 80, sums, 0.0))
    c0 = jnp.sum(jnp.where(lane1 == 81, sums, 0.0))
    alpha = jnp.full((1, 1), rho0, F32) / jnp.full((1, 1), c0, F32)
    image = partial + scatter(first.T, onehot) + forward(m2[:, 1, :].T)

    r1 = rhs - alpha * q0
    z1 = z0 - alpha * w0
    y1 = q0 - alpha * image
    rho1_part, c1_part, e1_part = jnp.sum(r1 * z1), jnp.sum(z1 * y1), jnp.sum(z1 * q0)
    s3[0] = jnp.where(
        lane1 == 0, rho1_part, jnp.where(lane1 == 1, c1_part, jnp.where(lane1 == 2, e1_part, 0.0))
    )
    exchange(3, s3, m3, one=True)
    arrived(3, m3)
    sums = jnp.sum(m3[:, 0, :], axis=0, keepdims=True)
    rho1, c1, e1 = (
        jnp.full((1, 1), jnp.sum(jnp.where(lane1 == i, sums, 0.0)), F32) for i in range(3)
    )
    beta = rho1 / jnp.full((1, 1), rho0, F32)
    step = rho1 / (c1 + 2.0 * beta * e1 + beta * beta * jnp.full((1, 1), c0, F32))
    x_ref[...] = alpha * z0 + step * (z1 + beta * z0)
    r_ref[...] = r1 - step * (y1 + beta * q0)
    for n, src in ((0, s0), (1, s1), (2, s2), (3, m3)):
        pltpu.make_async_copy(src.at[0 : N - 1], src.at[0 : N - 1], send.at[n]).wait()


def solve(right_side, diag_blocks, precond, upper_blocks, block_cols, slot_of_camera):
    shape = jax.ShapeDtypeStruct((B, N), F32)
    any_space = pl.BlockSpec(memory_space=pl.ANY)
    vmem = pl.BlockSpec(memory_space=pltpu.VMEM)
    row, two = pltpu.VMEM((N, 1, N), F32), pltpu.VMEM((N, 2, N), F32)
    return pl.pallas_call(
        kernel,
        out_shape=(shape, shape),
        in_specs=[any_space] * 6,
        out_specs=(vmem, vmem),
        scratch_shapes=[
            pltpu.VMEM((B, N), F32),
            pltpu.VMEM((B, B, N), F32),
            pltpu.VMEM((B, B, N), F32),
            pltpu.VMEM((B, B, K, N), F32),
            pltpu.VMEM((K, N), I32),
            pltpu.VMEM((N, N), I32),
            pltpu.SemaphoreType.DMA((6,)),
            row, row, row, row, two, two, pltpu.VMEM((1, 1, N), F32), row,
            pltpu.SemaphoreType.DMA((4,)),
            pltpu.SemaphoreType.DMA((4,)),
            pltpu.VMEM((K * B, N), F32),
            pltpu.VMEM((K * B, N), F32),
        ],
        compiler_params=pltpu.CompilerParams(collective_id=0, has_side_effects=True),
    )(
        right_side,
        diag_blocks,
        precond,
        jnp.transpose(upper_blocks, (1, 2, 0, 3)),
        block_cols,
        slot_of_camera.reshape(N, N),
    )


def solution(mesh):
    return jax.shard_map(
        solve,
        mesh=mesh,
        in_specs=(
            P(None, "rows"),
            P(None, None, "rows"),
            P(None, None, "rows"),
            P(None, None, None, "rows"),
            P(None, "rows"),
            P(),
        ),
        out_specs=(P(None, "rows"), P(None, "rows")),
        check_vma=False,
    )
```

```python
import functools
import itertools

import jax
import jax.numpy as jnp
from jax import lax
from jax.experimental import pallas as pl
from jax.experimental.pallas import tpu as pltpu
from jax.sharding import PartitionSpec as P

MESH = pl.DeviceIdType.MESH
B = 9
K = 8
N = 128
F32, BF16, I32 = jnp.float32, jnp.bfloat16, jnp.int32


def hops(d):
    return sum(min(k, 4 - k) for k in d[:3])


STEPS = sorted(
    (d for d in itertools.product(range(4), range(4), range(4), range(2)) if any(d)),
    key=lambda d: -hops(d),
)


def targets(me):
    x, y, z, c = me // 32, lax.rem(me // 8, 4), lax.rem(me // 2, 4), lax.rem(me, 2)
    tx = [lax.rem(x + d, 4) * 32 for d in range(4)]
    ty = [lax.rem(y + d, 4) * 8 for d in range(4)]
    tz = [lax.rem(z + d, 4) * 2 for d in range(4)]
    tc = [c, 1 - c]
    xy = {(i, j): tx[i] + ty[j] for i in range(4) for j in range(4)}
    zc = {(i, j): tz[i] + tc[j] for i in range(4) for j in range(2)}
    return [xy[d[0], d[1]] + zc[d[2], d[3]] for d in STEPS]


def iota(shape, dim):
    return lax.broadcasted_iota(I32, shape, dim)


def lanes(x, idx):
    return jnp.take_along_axis(x, idx, axis=1, mode="promise_in_bounds")


def rows8(row):
    return jnp.broadcast_to(row, (K, N))


def pieces(x):
    hi = x.astype(BF16)
    rest = x - hi.astype(F32)
    mid = rest.astype(BF16)
    return hi, mid, (rest - mid.astype(F32)).astype(BF16)


def dot_t(a, b):
    return lax.dot_general(a, b, (((1,), (1,)), ((), ())), preferred_element_type=F32)


def blocks_times(m_ref, v):
    total = m_ref[0] * v[0:1]
    for a in range(1, B):
        total = total + m_ref[a] * v[a : a + 1]
    return total


def kernel(
    b_hbm, d_hbm, p_hbm, u_hbm, c_hbm, t_hbm, o_ref,
    b_v, d_v, p_v, u_v, c_v, t_v, in_sem,
    s0, m0, s1, m1, s2, m2, s3, m3, send, recv, pt, ft,
):
    me = lax.axis_index("rows")
    peers = targets(me)
    barrier = pltpu.get_barrier_semaphore()
    for t in peers:
        pl.semaphore_signal(barrier, inc=1, device_id=(t,), device_id_type=MESH)
    copies = [
        pltpu.make_async_copy(src, dst, in_sem.at[i])
        for i, (src, dst) in enumerate(
            [(c_hbm, c_v), (t_hbm, t_v), (b_hbm, b_v), (p_hbm, p_v), (u_hbm, u_v), (d_hbm, d_v)]
        )
    ]
    for c in copies:
        c.start()

    def exchange(n, src, dst, one=False):
        for t in peers:
            pltpu.make_async_remote_copy(
                src_ref=src.at[0 if one else t],
                dst_ref=dst.at[me],
                send_sem=send.at[n],
                recv_sem=recv.at[n],
                device_id=(t,),
                device_id_type=MESH,
            ).start()
        dst[me] = src[0] if one else src[me]

    def arrived(n, dst):
        pltpu.make_async_copy(dst.at[0 : N - 1], dst.at[0 : N - 1], recv.at[n]).wait()

    copies[0].wait()
    copies[1].wait()
    cams = c_v[...]
    hi, lo = cams >> 7, cams & 127
    slots = jnp.zeros((K, N), I32)
    for r in range(N):
        slots = jnp.where(hi == r, lanes(rows8(t_v[r : r + 1, :]), lo), slots)
    owner, offset = slots >> 7, slots & 127

    sub = iota((N, N), 0)
    picks = [sub == owner[k : k + 1, :] for k in range(K)]
    ones = [jnp.where(p, 1.0, 0.0).astype(BF16) for p in picks]
    by_owner = jnp.concatenate(ones, axis=1)
    before = jnp.where(sub < iota((N, N), 1), 1.0, 0.0).astype(BF16)
    stacked = jnp.concatenate(ones, axis=0)
    earlier = jnp.dot(stacked, before, preferred_element_type=F32)
    counts = jnp.dot(stacked, jnp.ones((N, N), BF16), preferred_element_type=F32)
    base = jnp.zeros((N, N), F32)
    ranks = []
    for k in range(K):
        here = earlier[k * N : (k + 1) * N] + base
        ranks.append(jnp.sum(jnp.where(picks[k], here, 0.0), axis=0, keepdims=True))
        base = base + counts[k * N : (k + 1) * N]
    rank = jnp.concatenate(ranks, axis=0).astype(I32)
    sub8 = iota((K, N), 0)
    places = [rank[k : k + 1, :] == sub8 for k in range(K)]

    def spread(v):
        out = []
        for b in range(B):
            total = u_v[0, b] * v[0:1]
            for a in range(1, B):
                total = total + u_v[a, b] * v[a : a + 1]
            out.append(total)
        return out

    def to_owners(lists):
        wide = jnp.concatenate(
            [
                jnp.concatenate(
                    [jnp.where(places[k], rows8(e[k : k + 1, :]), 0.0) for k in range(K)], axis=1
                )
                for e in lists
            ]
            + [jnp.zeros((N - K * len(lists), K * N), F32)],
            axis=0,
        )
        h, m, l = pieces(wide)
        return dot_t(by_owner, h) + dot_t(by_owner, m) + dot_t(by_owner, l)

    def answers(v, asked):
        parts = [lanes(rows8(v[b : b + 1]), asked) for b in range(B)]
        return jnp.concatenate(parts + [jnp.zeros((N - K * B, N), F32)], axis=0).T

    def scatter(got, onehot):
        pt[...] = got[0 : K * B]
        flat = jnp.concatenate([pt[pl.ds(r, B, stride=K), :] for r in range(K)], axis=1)
        h, m, l = pieces(flat)
        return dot_t(h, onehot) + dot_t(m, onehot) + dot_t(l, onehot)

    def forward(got):
        ft[...] = got[0 : K * B]
        total = [jnp.zeros((K, N), F32) for _ in range(B)]
        for b in range(B):
            g = jnp.zeros((K, N), F32)
            for r in range(K):
                row = rows8(ft[K * b + r : K * b + r + 1, :])
                g = jnp.where(rank == r, lanes(row, owner), g)
            for a in range(B):
                total[a] = total[a] + u_v[a, b] * g
        return jnp.concatenate([jnp.sum(t, axis=0, keepdims=True) for t in total], axis=0)

    copies[2].wait()
    copies[3].wait()
    rhs = b_v[...]
    z0 = blocks_times(p_v, rhs)
    copies[4].wait()
    copies[5].wait()
    s0[:, 0, :] = to_owners(spread(z0) + [offset.astype(F32)])
    pl.semaphore_wait(barrier, N - 1)
    exchange(0, s0, m0)

    lane = iota((N, N), 1)
    partial = blocks_times(d_v, z0)
    rho0_part = jnp.sum(rhs * z0)
    arrived(0, m0)
    got = m0[:, 0, :].T
    asked = got[K * B : K * B + K].astype(I32)
    s1[:, 0, :] = answers(z0, asked)
    exchange(1, s1, m1)
    onehot = jnp.concatenate(
        [jnp.where(sub == asked[r : r + 1, :], 1.0, 0.0).astype(BF16) for r in range(K)], axis=1
    )
    partial = partial + scatter(got, onehot)
    arrived(1, m1)
    q0 = partial + forward(m1[:, 0, :].T)

    w0 = blocks_times(p_v, q0)
    c0_part = jnp.sum(z0 * q0)
    out = to_owners(spread(w0))
    s2[:, 0, :] = jnp.where(lane == 80, rho0_part, jnp.where(lane == 81, c0_part, out))
    s2[:, 1, :] = answers(w0, asked)
    exchange(2, s2, m2)
    partial = blocks_times(d_v, w0)
    arrived(2, m2)
    first = m2[:, 0, :]
    sums = jnp.sum(first, axis=0, keepdims=True)
    lane1 = iota((1, N), 1)
    rho0 = jnp.sum(jnp.where(lane1 == 80, sums, 0.0))
    c0 = jnp.sum(jnp.where(lane1 == 81, sums, 0.0))
    alpha = jnp.full((1, 1), rho0, F32) / jnp.full((1, 1), c0, F32)
    image = partial + scatter(first.T, onehot) + forward(m2[:, 1, :].T)

    r1 = rhs - alpha * q0
    z1 = z0 - alpha * w0
    y1 = q0 - alpha * image
    rho1_part, c1_part, e1_part = jnp.sum(r1 * z1), jnp.sum(z1 * y1), jnp.sum(z1 * q0)
    s3[0] = jnp.where(
        lane1 == 0, rho1_part, jnp.where(lane1 == 1, c1_part, jnp.where(lane1 == 2, e1_part, 0.0))
    )
    exchange(3, s3, m3, one=True)
    arrived(3, m3)
    sums = jnp.sum(m3[:, 0, :], axis=0, keepdims=True)
    rho1, c1, e1 = (
        jnp.full((1, 1), jnp.sum(jnp.where(lane1 == i, sums, 0.0)), F32) for i in range(3)
    )
    beta = rho1 / jnp.full((1, 1), rho0, F32)
    step = rho1 / (c1 + 2.0 * beta * e1 + beta * beta * jnp.full((1, 1), c0, F32))
    o_ref[0] = alpha * z0 + step * (z1 + beta * z0)
    o_ref[1] = r1 - step * (y1 + beta * q0)
    for n, src in ((0, s0), (1, s1), (2, s2), (3, m3)):
        pltpu.make_async_copy(src.at[0 : N - 1], src.at[0 : N - 1], send.at[n]).wait()


def solve(right_side, diag_blocks, precond, upper_blocks, block_cols, slot_of_camera):
    shape = jax.ShapeDtypeStruct((B, N), F32)
    any_space = pl.BlockSpec(memory_space=pltpu.HBM)
    vmem = pl.BlockSpec(memory_space=pltpu.VMEM)
    row, two = pltpu.VMEM((N, 1, N), F32), pltpu.VMEM((N, 2, N), F32)
    out = pl.pallas_call(
        kernel,
        out_shape=jax.ShapeDtypeStruct((2, B, N), F32),
        in_specs=[any_space] * 6,
        out_specs=vmem,
        scratch_shapes=[
            pltpu.VMEM((B, N), F32),
            pltpu.VMEM((B, B, N), F32),
            pltpu.VMEM((B, B, N), F32),
            pltpu.VMEM((B, B, K, N), F32),
            pltpu.VMEM((K, N), I32),
            pltpu.VMEM((N, N), I32),
            pltpu.SemaphoreType.DMA((6,)),
            row, row, row, row, two, two, pltpu.VMEM((1, 1, N), F32), row,
            pltpu.SemaphoreType.DMA((4,)),
            pltpu.SemaphoreType.DMA((4,)),
            pltpu.VMEM((K * B, N), F32),
            pltpu.VMEM((K * B, N), F32),
        ],
        compiler_params=pltpu.CompilerParams(collective_id=0, has_side_effects=True, vmem_limit_bytes=8 << 20),
    )(
        *[
            pltpu.with_memory_space_constraint(x, pltpu.HBM)
            for x in (
                right_side,
                diag_blocks,
                precond,
                jnp.transpose(upper_blocks, (1, 2, 0, 3)),
                block_cols,
                slot_of_camera.reshape(N, N),
            )
        ]
    )
    return out[0], out[1]


def solution(mesh):
    return jax.shard_map(
        solve,
        mesh=mesh,
        in_specs=(
            P(None, "rows"),
            P(None, None, "rows"),
            P(None, None, "rows"),
            P(None, None, None, "rows"),
            P(None, "rows"),
            P(),
        ),
        out_specs=(P(None, "rows"), P(None, "rows")),
        check_vma=False,
    )
```

```python
import functools
import itertools

import jax
import jax.numpy as jnp
from jax import lax
from jax.experimental import pallas as pl
from jax.experimental.pallas import tpu as pltpu
from jax.sharding import PartitionSpec as P

MESH = pl.DeviceIdType.MESH
B = 9
K = 8
N = 128
CHIPS = N // 2
PLANE = 16
F32, BF16, I32 = jnp.float32, jnp.bfloat16, jnp.int32


def hops(d):
    return sum(min(k, 4 - k) for k in d[:3])


STEPS = sorted(
    (d for d in itertools.product(range(4), range(4), range(4), range(2)) if any(d)),
    key=lambda d: -hops(d),
)


def targets(me):
    x, y, z, c = me // 32, lax.rem(me // 8, 4), lax.rem(me // 2, 4), lax.rem(me, 2)
    tx = [lax.rem(x + d, 4) * 32 for d in range(4)]
    ty = [lax.rem(y + d, 4) * 8 for d in range(4)]
    tz = [lax.rem(z + d, 4) * 2 for d in range(4)]
    tc = [c, 1 - c]
    xy = {(i, j): tx[i] + ty[j] for i in range(4) for j in range(4)}
    zc = {(i, j): tz[i] + tc[j] for i in range(4) for j in range(2)}
    return {d: xy[d[0], d[1]] + zc[d[2], d[3]] for d in STEPS}


def place_of(device):
    return lax.rem(device, 2) * CHIPS + device // 2


def iota(shape, dim):
    return lax.broadcasted_iota(I32, shape, dim)


def lanes(x, idx):
    return jnp.take_along_axis(x, idx, axis=1, mode="promise_in_bounds")


def rows8(row):
    return jnp.broadcast_to(row, (K, N))


def pieces(x):
    hi = x.astype(BF16)
    rest = x - hi.astype(F32)
    mid = rest.astype(BF16)
    return hi, mid, (rest - mid.astype(F32)).astype(BF16)


def dot_t(a, b):
    return lax.dot_general(a, b, (((1,), (1,)), ((), ())), preferred_element_type=F32)


def blocks_times(m_ref, v):
    total = m_ref[0] * v[0:1]
    for a in range(1, B):
        total = total + m_ref[a] * v[a : a + 1]
    return total


def kernel(
    b_hbm, d_hbm, p_hbm, u_hbm, c_hbm, t_hbm, o_ref,
    b_v, d_v, p_v, u_v, c_v, t_v, in_sem,
    s0, m0, tile, tiles, s2, m2, s3, m3, send, recv, plane_recv, half_send, half_recv, pt, ft, wt, gt,
):
    me = lax.axis_index("rows")
    mine = place_of(me)
    core = lax.rem(me, 2)
    peers = targets(me)
    copies = [
        pltpu.make_async_copy(src, dst, in_sem.at[i])
        for i, (src, dst) in enumerate(
            [(c_hbm, c_v), (t_hbm, t_v), (b_hbm, b_v), (p_hbm, p_v), (u_hbm, u_v), (d_hbm, d_v)]
        )
    ]
    for c in copies:
        c.start()
    barrier = pltpu.get_barrier_semaphore()
    for d in STEPS:
        pl.semaphore_signal(barrier, inc=1, device_id=(peers[d],), device_id_type=MESH)

    def exchange(n, src, dst, one=False):
        for d in STEPS:
            pltpu.make_async_remote_copy(
                src_ref=src.at[0 if one else place_of(peers[d])],
                dst_ref=dst.at[mine],
                send_sem=send.at[n],
                recv_sem=recv.at[n],
                device_id=(peers[d],),
                device_id_type=MESH,
            ).start()
        dst[mine] = src[0] if one else src[mine]

    def arrived(n, dst):
        pltpu.make_async_copy(dst.at[0 : N - 1], dst.at[0 : N - 1], recv.at[n]).wait()

    def plane(dx, half):
        x = lax.rem(me // 32 - dx + 4, 4)
        return pl.ds(pl.multiple_of(half * CHIPS + x * PLANE, PLANE), PLANE)

    copies[0].wait()
    copies[1].wait()
    cams = c_v[...]
    hi, lo = cams >> 7, cams & 127
    slots = jnp.zeros((K, N), I32)
    for r in range(N):
        slots = jnp.where(hi == r, lanes(rows8(t_v[r : r + 1, :]), lo), slots)
    device, offset = slots >> 7, slots & 127
    owner = (device & 1) * CHIPS + (device >> 1)

    sub = iota((N, N), 0)
    picks = [sub == owner[k : k + 1, :] for k in range(K)]
    ones = [jnp.where(p, 1.0, 0.0).astype(BF16) for p in picks]
    by_owner = jnp.concatenate(ones, axis=1)
    before = jnp.where(sub < iota((N, N), 1), 1.0, 0.0).astype(BF16)
    stacked = jnp.concatenate(ones, axis=0)
    earlier = jnp.dot(stacked, before, preferred_element_type=F32)
    counts = jnp.dot(stacked, jnp.ones((N, N), BF16), preferred_element_type=F32)
    base = jnp.zeros((N, N), F32)
    ranks = []
    for k in range(K):
        here = earlier[k * N : (k + 1) * N] + base
        ranks.append(jnp.sum(jnp.where(picks[k], here, 0.0), axis=0, keepdims=True))
        base = base + counts[k * N : (k + 1) * N]
    rank = jnp.concatenate(ranks, axis=0).astype(I32)
    sub8 = iota((K, N), 0)
    places = [rank[k : k + 1, :] == sub8 for k in range(K)]

    def spread(v):
        out = []
        for b in range(B):
            total = u_v[0, b] * v[0:1]
            for a in range(1, B):
                total = total + u_v[a, b] * v[a : a + 1]
            out.append(total)
        return out

    def to_owners(lists):
        wide = jnp.concatenate(
            [
                jnp.concatenate(
                    [jnp.where(places[k], rows8(e[k : k + 1, :]), 0.0) for k in range(K)], axis=1
                )
                for e in lists
            ]
            + [jnp.zeros((N - K * len(lists), K * N), F32)],
            axis=0,
        )
        h, m, l = pieces(wide)
        return dot_t(by_owner, h) + dot_t(by_owner, m) + dot_t(by_owner, l)

    def answers(v, asked):
        parts = [lanes(rows8(v[b : b + 1]), asked) for b in range(B)]
        return jnp.concatenate(parts + [jnp.zeros((N - K * B, N), F32)], axis=0).T

    def scatter(got, onehot):
        pt[...] = got[0 : K * B]
        flat = jnp.concatenate([pt[pl.ds(r, B, stride=K), :] for r in range(K)], axis=1)
        h, m, l = pieces(flat)
        return dot_t(h, onehot) + dot_t(m, onehot) + dot_t(l, onehot)

    def forward(got):
        ft[...] = got[0 : K * B]
        total = [jnp.zeros((K, N), F32) for _ in range(B)]
        for b in range(B):
            g = jnp.zeros((K, N), F32)
            for r in range(K):
                row = rows8(ft[K * b + r : K * b + r + 1, :])
                g = jnp.where(rank == r, lanes(row, owner), g)
            for a in range(B):
                total[a] = total[a] + u_v[a, b] * g
        return jnp.concatenate([jnp.sum(t, axis=0, keepdims=True) for t in total], axis=0)

    copies[2].wait()
    copies[3].wait()
    rhs = b_v[...]
    z0 = blocks_times(p_v, rhs)
    tile[:, 0, :] = z0
    copies[4].wait()
    copies[5].wait()
    s0[:, 0, :] = to_owners(spread(z0) + [offset.astype(F32)])
    wanted = jnp.concatenate(
        [jnp.where(places[k], rows8(offset[k : k + 1, :]), 0).astype(F32) for k in range(K)], axis=1
    )
    wanted = jnp.concatenate([wanted] * (N // K), axis=0).astype(BF16)
    wanted = dot_t(by_owner, wanted).astype(I32)
    pl.semaphore_wait(barrier, N - 1)

    for dx in (2, 1, 3, 0):
        for d in STEPS:
            if d[0] == dx and d[3] == 0:
                pltpu.make_async_remote_copy(
                    src_ref=tile,
                    dst_ref=tiles.at[:, mine],
                    send_sem=send.at[1],
                    recv_sem=plane_recv.at[dx],
                    device_id=(peers[d],),
                    device_id_type=MESH,
                ).start()
    exchange(0, s0, m0)
    tiles[:, mine] = tile[...]

    lane = iota((N, N), 1)
    partial = blocks_times(d_v, z0)
    rho0_part = jnp.sum(rhs * z0)
    halves = []
    for dx in (0, 1, 3, 2):
        n = PLANE - (dx == 0)
        pltpu.make_async_copy(tiles.at[:, 0:n], tiles.at[:, 0:n], plane_recv.at[dx]).wait()
        here = tiles.at[:, plane(dx, core)]
        halves.append(
            pltpu.make_async_remote_copy(
                src_ref=here,
                dst_ref=here,
                send_sem=half_send.at[dx],
                recv_sem=half_recv.at[dx],
                device_id=(peers[0, 0, 0, 1],),
                device_id_type=MESH,
            )
        )
        halves[-1].start()

    block = iota((PLANE, N), 1) >> 3
    wt[...] = wanted

    def pick(dx, half):
        where = plane(dx, half)
        index = wt[where, :]
        out = jnp.zeros((PLANE, N), F32)
        for b in range(B):
            z = tiles[b, where, 0, :]
            g = jnp.concatenate([lanes(z[i : i + K], index[i : i + K]) for i in (0, K)], axis=0)
            out = jnp.where(block == b, g, out)
        gt[where, :] = out

    for dx in (0, 1, 3, 2):
        pick(dx, core)
    arrived(0, m0)
    got = m0[:, 0, :].T
    asked = got[K * B : K * B + K].astype(I32)
    onehot = jnp.concatenate(
        [jnp.where(sub == asked[r : r + 1, :], 1.0, 0.0).astype(BF16) for r in range(K)], axis=1
    )
    partial = partial + scatter(got, onehot)
    for n, dx in enumerate((0, 1, 3, 2)):
        halves[n].wait_recv()
        pick(dx, 1 - core)
    q0 = partial + forward(gt[...].T)

    w0 = blocks_times(p_v, q0)
    c0_part = jnp.sum(z0 * q0)
    out = to_owners(spread(w0))
    s2[:, 0, :] = jnp.where(lane == 80, rho0_part, jnp.where(lane == 81, c0_part, out))
    s2[:, 1, :] = answers(w0, asked)
    exchange(2, s2, m2)
    partial = blocks_times(d_v, w0)
    arrived(2, m2)
    first = m2[:, 0, :]
    sums = jnp.sum(first, axis=0, keepdims=True)
    lane1 = iota((1, N), 1)
    rho0 = jnp.sum(jnp.where(lane1 == 80, sums, 0.0))
    c0 = jnp.sum(jnp.where(lane1 == 81, sums, 0.0))
    alpha = jnp.full((1, 1), rho0, F32) / jnp.full((1, 1), c0, F32)
    image = partial + scatter(first.T, onehot) + forward(m2[:, 1, :].T)

    r1 = rhs - alpha * q0
    z1 = z0 - alpha * w0
    y1 = q0 - alpha * image
    rho1_part, c1_part, e1_part = jnp.sum(r1 * z1), jnp.sum(z1 * y1), jnp.sum(z1 * q0)
    s3[0] = jnp.where(
        lane1 == 0, rho1_part, jnp.where(lane1 == 1, c1_part, jnp.where(lane1 == 2, e1_part, 0.0))
    )
    exchange(3, s3, m3, one=True)
    arrived(3, m3)
    sums = jnp.sum(m3[:, 0, :], axis=0, keepdims=True)
    rho1, c1, e1 = (
        jnp.full((1, 1), jnp.sum(jnp.where(lane1 == i, sums, 0.0)), F32) for i in range(3)
    )
    beta = rho1 / jnp.full((1, 1), rho0, F32)
    step = rho1 / (c1 + 2.0 * beta * e1 + beta * beta * jnp.full((1, 1), c0, F32))
    o_ref[0] = alpha * z0 + step * (z1 + beta * z0)
    o_ref[1] = r1 - step * (y1 + beta * q0)
    for n, src in ((0, m0), (2, m2), (3, m3)):
        pltpu.make_async_copy(src.at[0 : N - 1], src.at[0 : N - 1], send.at[n]).wait()
    pltpu.make_async_copy(
        tiles.at[:, 0 : CHIPS - 1], tiles.at[:, 0 : CHIPS - 1], send.at[1]
    ).wait()
    for h in halves:
        h.wait_send()


def solve(right_side, diag_blocks, precond, upper_blocks, block_cols, slot_of_camera):
    shape = jax.ShapeDtypeStruct((B, N), F32)
    any_space = pl.BlockSpec(memory_space=pltpu.HBM)
    vmem = pl.BlockSpec(memory_space=pltpu.VMEM)
    row, two = pltpu.VMEM((N, 1, N), F32), pltpu.VMEM((N, 2, N), F32)
    out = pl.pallas_call(
        kernel,
        out_shape=jax.ShapeDtypeStruct((2, B, N), F32),
        in_specs=[any_space] * 6,
        out_specs=vmem,
        scratch_shapes=[
            pltpu.VMEM((B, N), F32),
            pltpu.VMEM((B, B, N), F32),
            pltpu.VMEM((B, B, N), F32),
            pltpu.VMEM((B, B, K, N), F32),
            pltpu.VMEM((K, N), I32),
            pltpu.VMEM((N, N), I32),
            pltpu.SemaphoreType.DMA((6,)),
            row, row, pltpu.VMEM((B, 1, N), F32), pltpu.VMEM((B, N, 1, N), F32),
            two, two, pltpu.VMEM((1, 1, N), F32), row,
            *[pltpu.SemaphoreType.DMA((4,))] * 5,
            pltpu.VMEM((K * B, N), F32),
            pltpu.VMEM((K * B, N), F32),
            pltpu.VMEM((N, N), I32),
            pltpu.VMEM((N, N), F32),
        ],
        compiler_params=pltpu.CompilerParams(collective_id=0, has_side_effects=True, vmem_limit_bytes=8 << 20),
    )(
        *[
            pltpu.with_memory_space_constraint(x, pltpu.HBM)
            for x in (
                right_side,
                diag_blocks,
                precond,
                jnp.transpose(upper_blocks, (1, 2, 0, 3)),
                block_cols,
                slot_of_camera.reshape(N, N),
            )
        ]
    )
    return out[0], out[1]


def solution(mesh):
    return jax.shard_map(
        solve,
        mesh=mesh,
        in_specs=(
            P(None, "rows"),
            P(None, None, "rows"),
            P(None, None, "rows"),
            P(None, None, None, "rows"),
            P(None, "rows"),
            P(),
        ),
        out_specs=(P(None, "rows"), P(None, "rows")),
        check_vma=False,
    )
```

```python
import functools
import itertools

import jax
import jax.numpy as jnp
from jax import lax
from jax.experimental import pallas as pl
from jax.experimental.pallas import tpu as pltpu
from jax.sharding import PartitionSpec as P

MESH = pl.DeviceIdType.MESH
B = 9
K = 8
N = 128
CHIPS = N // 2
PLANE = 16
F32, BF16, I32 = jnp.float32, jnp.bfloat16, jnp.int32


def hops(d):
    return sum(min(k, 4 - k) for k in d[:3])


STEPS = sorted(
    (d for d in itertools.product(range(4), range(4), range(4), range(2)) if any(d)),
    key=lambda d: -hops(d),
)


class Peers:
    def __init__(self, me):
        x, y, z, c = me // 32, lax.rem(me // 8, 4), lax.rem(me // 2, 4), lax.rem(me, 2)
        self.x = [lax.rem(x + d, 4) * 16 for d in range(4)]
        self.yz = [[lax.rem(y + i, 4) * 4 + lax.rem(z + j, 4) for j in range(4)] for i in range(4)]
        self.core = [c, 1 - c]
        self.half = [c * CHIPS, CHIPS - c * CHIPS]

    def chip(self, d):
        return self.x[d[0]] + self.yz[d[1]][d[2]]

    def device(self, d):
        return self.chip(d) * 2 + self.core[d[3]]

    def place(self, d):
        return self.chip(d) + self.half[d[3]]


def place_of(device):
    return lax.rem(device, 2) * CHIPS + device // 2


def iota(shape, dim):
    return lax.broadcasted_iota(I32, shape, dim)


def lanes(x, idx):
    return jnp.take_along_axis(x, idx, axis=1, mode="promise_in_bounds")


def rows8(row):
    return jnp.broadcast_to(row, (K, N))


def pieces(x):
    hi = x.astype(BF16)
    rest = x - hi.astype(F32)
    mid = rest.astype(BF16)
    return hi, mid, (rest - mid.astype(F32)).astype(BF16)


def total(x):
    rows = jnp.sum(x, axis=0, keepdims=True)
    return jnp.sum(rows, axis=1, keepdims=True)


def dot_t(a, b):
    return lax.dot_general(a, b, (((1,), (1,)), ((), ())), preferred_element_type=F32)


def blocks_times(m_ref, v):
    total = m_ref[0] * v[0:1]
    for a in range(1, B):
        total = total + m_ref[a] * v[a : a + 1]
    return total


def kernel(
    b_hbm, d_hbm, p_hbm, u_hbm, c_hbm, t_hbm, o_ref,
    b_v, d_v, p_v, u_v, c_v, t_v, in_sem,
    s0, m0, tile, tiles, s2, m2, s3, m3, send, recv, plane_recv, half_send, half_recv, pt, ft, wt, gt,
):
    me = lax.axis_index("rows")
    mine = place_of(me)
    core = lax.rem(me, 2)
    peers = Peers(me)
    barrier = pltpu.get_barrier_semaphore()

    def greet(steps):
        for d in steps:
            pl.semaphore_signal(
                barrier, inc=1, device_id=(peers.device(d),), device_id_type=MESH
            )

    far = [d for d in STEPS if hops(d) > 4]
    greet(far)
    copies = [
        pltpu.make_async_copy(src, dst, in_sem.at[i])
        for i, (src, dst) in enumerate(
            [(c_hbm, c_v), (t_hbm, t_v), (b_hbm, b_v), (p_hbm, p_v), (u_hbm, u_v), (d_hbm, d_v)]
        )
    ]
    for c in copies:
        c.start()
    greet(STEPS[len(far) :])

    def exchange(n, src, dst, rows=1, one=False):
        def of(ref, place):
            return ref.at[pl.ds(place * rows, rows)]

        for d in STEPS:
            pltpu.make_async_remote_copy(
                src_ref=src if one else of(src, peers.place(d)),
                dst_ref=of(dst, mine),
                send_sem=send.at[n],
                recv_sem=recv.at[n],
                device_id=(peers.device(d),),
                device_id_type=MESH,
            ).start()
        own = pl.ds(mine * rows, rows)
        dst[own, :] = src[...] if one else src[own, :]

    def arrived(n, dst, rows=1):
        most = dst.at[0 : rows * (N - 1)]
        pltpu.make_async_copy(most, most, recv.at[n]).wait()

    def plane(dx, half):
        x = lax.rem(me // 32 - dx + 4, 4)
        return pl.ds(pl.multiple_of(half * CHIPS + x * PLANE, PLANE), PLANE)

    copies[0].wait()
    copies[1].wait()
    cams = c_v[...]
    hi, lo = cams >> 7, cams & 127
    slots = jnp.zeros((K, N), I32)
    for r in range(N):
        slots = jnp.where(hi == r, lanes(rows8(t_v[r : r + 1, :]), lo), slots)
    device, offset = slots >> 7, slots & 127
    owner = (device & 1) * CHIPS + (device >> 1)

    sub = iota((N, N), 0)
    picks = [sub == owner[k : k + 1, :] for k in range(K)]
    ones = [jnp.where(p, 1.0, 0.0).astype(BF16) for p in picks]
    by_owner = jnp.concatenate(ones, axis=1)
    before = jnp.where(sub < iota((N, N), 1), 1.0, 0.0).astype(BF16)
    stacked = jnp.concatenate(ones, axis=0)
    earlier = jnp.dot(stacked, before, preferred_element_type=F32)
    counts = jnp.dot(stacked, jnp.ones((N, N), BF16), preferred_element_type=F32)
    base = jnp.zeros((N, N), F32)
    ranks = []
    for k in range(K):
        here = earlier[k * N : (k + 1) * N] + base
        ranks.append(jnp.sum(jnp.where(picks[k], here, 0.0), axis=0, keepdims=True))
        base = base + counts[k * N : (k + 1) * N]
    rank = jnp.concatenate(ranks, axis=0).astype(I32)
    sub8 = iota((K, N), 0)
    places = [rank[k : k + 1, :] == sub8 for k in range(K)]

    def spread(v):
        out = []
        for b in range(B):
            total = u_v[0, b] * v[0:1]
            for a in range(1, B):
                total = total + u_v[a, b] * v[a : a + 1]
            out.append(total)
        return out

    def to_owners(lists):
        wide = jnp.concatenate(
            [
                jnp.concatenate(
                    [jnp.where(places[k], rows8(e[k : k + 1, :]), 0.0) for k in range(K)], axis=1
                )
                for e in lists
            ]
            + [jnp.zeros((N - K * len(lists), K * N), F32)],
            axis=0,
        )
        h, m, l = pieces(wide)
        both = dot_t(by_owner, jnp.concatenate([h, m], axis=0))
        return both[:, 0:N] + both[:, N:] + dot_t(by_owner, l)

    def answers(v, asked):
        parts = [lanes(rows8(v[b : b + 1]), asked) for b in range(B)]
        return jnp.concatenate(parts + [jnp.zeros((N - K * B, N), F32)], axis=0).T

    def scatter(got, onehot):
        pt[...] = got
        flat = jnp.concatenate([pt[pl.ds(r, 16, stride=K), :] for r in range(K)], axis=1)
        out = dot_t(jnp.concatenate(pieces(flat), axis=0), onehot)
        return out[0:B] + out[16 : 16 + B] + out[32 : 32 + B]

    def forward(got):
        ft[...] = got[0 : K * B]
        total = [jnp.zeros((K, N), F32) for _ in range(B)]
        for b in range(B):
            g = jnp.zeros((K, N), F32)
            for r in range(K):
                row = rows8(ft[K * b + r : K * b + r + 1, :])
                g = jnp.where(rank == r, lanes(row, owner), g)
            for a in range(B):
                total[a] = total[a] + u_v[a, b] * g
        return jnp.concatenate([jnp.sum(t, axis=0, keepdims=True) for t in total], axis=0)

    copies[2].wait()
    copies[3].wait()
    rhs = b_v[...]
    z0 = blocks_times(p_v, rhs)
    tile[...] = z0
    copies[4].wait()
    copies[5].wait()
    s0[...] = to_owners(spread(z0) + [offset.astype(F32)])
    wanted = jnp.concatenate(
        [jnp.where(places[k], rows8(offset[k : k + 1, :]), 0).astype(F32) for k in range(K)], axis=1
    )
    wanted = jnp.concatenate([wanted] * (N // K), axis=0).astype(BF16)
    wanted = dot_t(by_owner, wanted).astype(I32)
    pl.semaphore_wait(barrier, N - 1)

    for dx in (2, 1, 3, 0):
        for d in STEPS:
            if d[0] == dx and d[3] == 0:
                pltpu.make_async_remote_copy(
                    src_ref=tile,
                    dst_ref=tiles.at[:, mine],
                    send_sem=send.at[1],
                    recv_sem=plane_recv.at[dx],
                    device_id=(peers.device(d),),
                    device_id_type=MESH,
                ).start()
    exchange(0, s0, m0)
    tiles[:, mine] = tile[...]

    lane = iota((N, N), 1)
    partial = blocks_times(d_v, z0)
    rho0_part = total(rhs * z0)
    halves = []
    for dx in (0, 1, 3, 2):
        n = PLANE - (dx == 0)
        pltpu.make_async_copy(tiles.at[:, 0:n], tiles.at[:, 0:n], plane_recv.at[dx]).wait()
        here = tiles.at[:, plane(dx, core)]
        halves.append(
            pltpu.make_async_remote_copy(
                src_ref=here,
                dst_ref=here,
                send_sem=half_send.at[dx],
                recv_sem=half_recv.at[dx],
                device_id=(peers.device((0, 0, 0, 1)),),
                device_id_type=MESH,
            )
        )
        halves[-1].start()

    block = iota((PLANE, N), 1) >> 3
    wt[...] = wanted

    def pick(dx, half):
        where = plane(dx, half)
        index = wt[where, :]
        out = jnp.zeros((PLANE, N), F32)
        for b in range(B):
            z = tiles[b, where, :]
            g = jnp.concatenate([lanes(z[i : i + K], index[i : i + K]) for i in (0, K)], axis=0)
            out = jnp.where(block == b, g, out)
        gt[where, :] = out

    for dx in (0, 1, 3, 2):
        pick(dx, core)
    arrived(0, m0)
    got = m0[...].T
    asked = got[K * B : K * B + K].astype(I32)
    onehot = jnp.concatenate(
        [jnp.where(sub == asked[r : r + 1, :], 1.0, 0.0).astype(BF16) for r in range(K)], axis=1
    )
    partial = partial + scatter(got, onehot)
    for n, dx in enumerate((0, 1, 3, 2)):
        halves[n].wait_recv()
        pick(dx, 1 - core)
    q0 = partial + forward(gt[...].T)

    w0 = blocks_times(p_v, q0)
    even, odd = pl.ds(0, N, stride=2), pl.ds(1, N, stride=2)
    s2[odd, :] = answers(w0, asked)
    c0_part = total(z0 * q0)
    out = to_owners(spread(w0))
    s2[even, :] = jnp.where(lane == 80, rho0_part, jnp.where(lane == 81, c0_part, out))
    exchange(2, s2, m2, rows=2)
    partial = blocks_times(d_v, w0)
    arrived(2, m2, rows=2)
    first = m2[even, :]
    sums = jnp.sum(first, axis=0, keepdims=True)
    lane1 = iota((1, N), 1)
    rho0, c0 = (total(jnp.where(lane1 == i, sums, 0.0)) for i in (80, 81))
    alpha = rho0 / c0
    image = partial + forward(m2[odd, :].T) + scatter(first.T, onehot)

    r1 = rhs - alpha * q0
    z1 = z0 - alpha * w0
    y1 = q0 - alpha * image
    rho1_part, c1_part, e1_part = total(r1 * z1), total(z1 * y1), total(z1 * q0)
    s3[...] = jnp.where(
        lane1 == 0, rho1_part, jnp.where(lane1 == 1, c1_part, jnp.where(lane1 == 2, e1_part, 0.0))
    )
    exchange(3, s3, m3, one=True)
    arrived(3, m3)
    sums = jnp.sum(m3[...], axis=0, keepdims=True)
    rho1, c1, e1 = (total(jnp.where(lane1 == i, sums, 0.0)) for i in range(3))
    beta = rho1 / rho0
    step = rho1 / (c1 + 2.0 * beta * e1 + beta * beta * c0)
    o_ref[0] = alpha * z0 + step * (z1 + beta * z0)
    o_ref[1] = r1 - step * (y1 + beta * q0)
    for n, dst, rows in ((0, m0, 1), (2, m2, 2), (3, m3, 1)):
        most = dst.at[0 : rows * (N - 1)]
        pltpu.make_async_copy(most, most, send.at[n]).wait()
    pltpu.make_async_copy(
        tiles.at[:, 0 : CHIPS - 1], tiles.at[:, 0 : CHIPS - 1], send.at[1]
    ).wait()
    for h in halves:
        h.wait_send()


def solve(right_side, diag_blocks, precond, upper_blocks, block_cols, slot_of_camera):
    shape = jax.ShapeDtypeStruct((B, N), F32)
    any_space = pl.BlockSpec(memory_space=pltpu.HBM)
    vmem = pl.BlockSpec(memory_space=pltpu.VMEM)
    row, two = pltpu.VMEM((N, N), F32), pltpu.VMEM((2 * N, N), F32)
    out = pl.pallas_call(
        kernel,
        out_shape=jax.ShapeDtypeStruct((2, B, N), F32),
        in_specs=[any_space] * 6,
        out_specs=vmem,
        scratch_shapes=[
            pltpu.VMEM((B, N), F32),
            pltpu.VMEM((B, B, N), F32),
            pltpu.VMEM((B, B, N), F32),
            pltpu.VMEM((B, B, K, N), F32),
            pltpu.VMEM((K, N), I32),
            pltpu.VMEM((N, N), I32),
            pltpu.SemaphoreType.DMA((6,)),
            row, row, pltpu.VMEM((B, N), F32), pltpu.VMEM((B, N, N), F32),
            two, two, pltpu.VMEM((1, N), F32), row,
            *[pltpu.SemaphoreType.DMA((4,))] * 5,
            pltpu.VMEM((N, N), F32),
            pltpu.VMEM((K * B, N), F32),
            pltpu.VMEM((N, N), I32),
            pltpu.VMEM((N, N), F32),
        ],
        compiler_params=pltpu.CompilerParams(collective_id=0, has_side_effects=True, vmem_limit_bytes=8 << 20),
    )(
        *[
            pltpu.with_memory_space_constraint(x, pltpu.HBM)
            for x in (
                right_side,
                diag_blocks,
                precond,
                jnp.transpose(upper_blocks, (1, 2, 0, 3)),
                block_cols,
                slot_of_camera.reshape(N, N),
            )
        ]
    )
    return out[0], out[1]


def solution(mesh):
    return jax.shard_map(
        solve,
        mesh=mesh,
        in_specs=(
            P(None, "rows"),
            P(None, None, "rows"),
            P(None, None, "rows"),
            P(None, None, None, "rows"),
            P(None, "rows"),
            P(),
        ),
        out_specs=(P(None, "rows"), P(None, "rows")),
        check_vma=False,
    )
```

```python
import functools
import itertools

import jax
import jax.numpy as jnp
from jax import lax
from jax.experimental import pallas as pl
from jax.experimental.pallas import tpu as pltpu
from jax.sharding import PartitionSpec as P

MESH = pl.DeviceIdType.MESH
B = 9
K = 8
N = 128
CHIPS = N // 2
PLANE = 16
F32, BF16, I32 = jnp.float32, jnp.bfloat16, jnp.int32


def hops(d):
    return sum(min(k, 4 - k) for k in d[:3])


STEPS = sorted(
    (d for d in itertools.product(range(4), range(4), range(4), range(2)) if any(d)),
    key=lambda d: -hops(d),
)


class Peers:
    def __init__(self, me):
        x, y, z, c = me // 32, lax.rem(me // 8, 4), lax.rem(me // 2, 4), lax.rem(me, 2)
        self.x = [lax.rem(x + d, 4) * 16 for d in range(4)]
        self.yz = [[lax.rem(y + i, 4) * 4 + lax.rem(z + j, 4) for j in range(4)] for i in range(4)]
        self.core = [c, 1 - c]
        self.half = [c * CHIPS, CHIPS - c * CHIPS]

    def chip(self, d):
        return self.x[d[0]] + self.yz[d[1]][d[2]]

    def device(self, d):
        return self.chip(d) * 2 + self.core[d[3]]

    def place(self, d):
        return self.chip(d) + self.half[d[3]]


def place_of(device):
    return lax.rem(device, 2) * CHIPS + device // 2


def iota(shape, dim):
    return lax.broadcasted_iota(I32, shape, dim)


def lanes(x, idx):
    return jnp.take_along_axis(x, idx, axis=1, mode="promise_in_bounds")


def rows8(row):
    return jnp.broadcast_to(row, (K, N))


def pieces(x):
    hi = x.astype(BF16)
    rest = x - hi.astype(F32)
    mid = rest.astype(BF16)
    return hi, mid, (rest - mid.astype(F32)).astype(BF16)


def total(x):
    rows = jnp.sum(x, axis=0, keepdims=True)
    return jnp.sum(rows, axis=1, keepdims=True)


def dot_t(a, b):
    return lax.dot_general(a, b, (((1,), (1,)), ((), ())), preferred_element_type=F32)


def blocks_times(m_ref, v):
    total = m_ref[0] * v[0:1]
    for a in range(1, B):
        total = total + m_ref[a] * v[a : a + 1]
    return total


def kernel(
    b_hbm, d_hbm, p_hbm, u_hbm, c_hbm, t_hbm, o_ref,
    b_v, d_v, p_v, u_v, c_v, t_v, in_sem,
    s0, m0, tile, tiles, s2, m2, s3, m3, send, recv, plane_recv, half_send, half_recv, pt, ft, wt, gt,
):
    me = lax.axis_index("rows")
    mine = place_of(me)
    core = lax.rem(me, 2)
    peers = Peers(me)
    barrier = pltpu.get_barrier_semaphore()

    def greet(steps):
        for d in steps:
            pl.semaphore_signal(
                barrier, inc=1, device_id=(peers.device(d),), device_id_type=MESH
            )

    far = [d for d in STEPS if hops(d) > 4]
    greet(far)
    copies = [
        pltpu.make_async_copy(src, dst, in_sem.at[i])
        for i, (src, dst) in enumerate(
            [(c_hbm, c_v), (t_hbm, t_v), (b_hbm, b_v), (p_hbm, p_v), (u_hbm, u_v), (d_hbm, d_v)]
        )
    ]
    for c in copies:
        c.start()
    greet(STEPS[len(far) :])

    def exchange(n, src, dst, rows=1, one=False):
        def of(ref, place):
            return ref.at[pl.ds(place * rows, rows)]

        for d in STEPS:
            pltpu.make_async_remote_copy(
                src_ref=src if one else of(src, peers.place(d)),
                dst_ref=of(dst, mine),
                send_sem=send.at[n],
                recv_sem=recv.at[n],
                device_id=(peers.device(d),),
                device_id_type=MESH,
            ).start()
        own = pl.ds(mine * rows, rows)
        dst[own, :] = src[...] if one else src[own, :]

    def arrived(n, dst, rows=1):
        most = dst.at[0 : rows * (N - 1)]
        pltpu.make_async_copy(most, most, recv.at[n]).wait()

    def plane(dx, half):
        x = lax.rem(me // 32 - dx + 4, 4)
        return pl.ds(pl.multiple_of(half * CHIPS + x * PLANE, PLANE), PLANE)

    copies[0].wait()
    copies[1].wait()
    cams = c_v[...]
    hi, lo = cams >> 7, cams & 127
    slots = jnp.zeros((K, N), I32)
    for r in range(N):
        slots = jnp.where(hi == r, lanes(rows8(t_v[r : r + 1, :]), lo), slots)
    device, offset = slots >> 7, slots & 127
    owner = (device & 1) * CHIPS + (device >> 1)

    sub = iota((N, N), 0)
    picks = [sub == owner[k : k + 1, :] for k in range(K)]
    ones = [jnp.where(p, 1.0, 0.0).astype(BF16) for p in picks]
    by_owner = jnp.concatenate(ones, axis=1)
    before = jnp.where(sub < iota((N, N), 1), 1.0, 0.0).astype(BF16)
    stacked = jnp.concatenate(ones, axis=0)
    earlier = jnp.dot(stacked, before, preferred_element_type=F32)
    counts = jnp.dot(stacked, jnp.ones((N, N), BF16), preferred_element_type=F32)
    base = jnp.zeros((N, N), F32)
    ranks = []
    for k in range(K):
        here = earlier[k * N : (k + 1) * N] + base
        ranks.append(jnp.sum(jnp.where(picks[k], here, 0.0), axis=0, keepdims=True))
        base = base + counts[k * N : (k + 1) * N]
    rank = jnp.concatenate(ranks, axis=0).astype(I32)
    sub8 = iota((K, N), 0)
    places = [rank[k : k + 1, :] == sub8 for k in range(K)]

    def spread(v):
        out = []
        for b in range(B):
            total = u_v[0, b] * v[0:1]
            for a in range(1, B):
                total = total + u_v[a, b] * v[a : a + 1]
            out.append(total)
        return out

    which = jnp.concatenate(
        [
            jnp.concatenate([jnp.where(p, float(k), 0.0) for k, p in enumerate(places)], axis=1),
            jnp.concatenate([jnp.where(p, iota((K, N), 1), 0).astype(F32) for p in places], axis=1),
        ],
        axis=0,
    )
    which = dot_t(which.astype(BF16), by_owner).astype(I32)
    list_at, slot_at = which[0:K], which[K : 2 * K]

    def bucket(e):
        out = lanes(rows8(e[0:1, :]), slot_at)
        for k in range(1, K):
            out = jnp.where(list_at == k, lanes(rows8(e[k : k + 1, :]), slot_at), out)
        return out

    def to_owners(lists):
        rest = jnp.zeros((N - K * len(lists), N), F32)
        return jnp.concatenate(lists + [rest] if rest.shape[0] else lists, axis=0).T

    def answers(v, asked):
        parts = [lanes(rows8(v[b : b + 1]), asked) for b in range(B)]
        return jnp.concatenate(parts + [jnp.zeros((N - K * B, N), F32)], axis=0).T

    def scatter(got, onehot):
        pt[...] = got
        flat = jnp.concatenate([pt[pl.ds(r, 16, stride=K), :] for r in range(K)], axis=1)
        out = dot_t(jnp.concatenate(pieces(flat), axis=0), onehot)
        return out[0:B] + out[16 : 16 + B] + out[32 : 32 + B]

    def forward(got):
        ft[...] = got[0 : K * B]
        total = [jnp.zeros((K, N), F32) for _ in range(B)]
        for b in range(B):
            g = jnp.zeros((K, N), F32)
            for r in range(K):
                row = rows8(ft[K * b + r : K * b + r + 1, :])
                g = jnp.where(rank == r, lanes(row, owner), g)
            for a in range(B):
                total[a] = total[a] + u_v[a, b] * g
        return jnp.concatenate([jnp.sum(t, axis=0, keepdims=True) for t in total], axis=0)

    copies[2].wait()
    copies[3].wait()
    rhs = b_v[...]
    z0 = blocks_times(p_v, rhs)
    tile[...] = z0
    copies[4].wait()
    copies[5].wait()
    bucket_offset = bucket(offset.astype(F32))
    s0[...] = to_owners([bucket(e) for e in spread(z0)] + [bucket_offset])
    wanted = to_owners([bucket_offset] * (N // K)).astype(I32)
    pl.semaphore_wait(barrier, N - 1)

    for dx in (2, 1, 3, 0):
        for d in STEPS:
            if d[0] == dx and d[3] == 0:
                pltpu.make_async_remote_copy(
                    src_ref=tile,
                    dst_ref=tiles.at[:, mine],
                    send_sem=send.at[1],
                    recv_sem=plane_recv.at[dx],
                    device_id=(peers.device(d),),
                    device_id_type=MESH,
                ).start()
    exchange(0, s0, m0)
    tiles[:, mine] = tile[...]

    lane = iota((N, N), 1)
    partial = blocks_times(d_v, z0)
    rho0_part = total(rhs * z0)
    halves = []
    for dx in (0, 1, 3, 2):
        n = PLANE - (dx == 0)
        pltpu.make_async_copy(tiles.at[:, 0:n], tiles.at[:, 0:n], plane_recv.at[dx]).wait()
        here = tiles.at[:, plane(dx, core)]
        halves.append(
            pltpu.make_async_remote_copy(
                src_ref=here,
                dst_ref=here,
                send_sem=half_send.at[dx],
                recv_sem=half_recv.at[dx],
                device_id=(peers.device((0, 0, 0, 1)),),
                device_id_type=MESH,
            )
        )
        halves[-1].start()

    block = iota((PLANE, N), 1) >> 3
    wt[...] = wanted

    def pick(dx, half):
        where = plane(dx, half)
        index = wt[where, :]
        out = jnp.zeros((PLANE, N), F32)
        for b in range(B):
            z = tiles[b, where, :]
            g = jnp.concatenate([lanes(z[i : i + K], index[i : i + K]) for i in (0, K)], axis=0)
            out = jnp.where(block == b, g, out)
        gt[where, :] = out

    for dx in (0, 1, 3, 2):
        pick(dx, core)
    arrived(0, m0)
    got = m0[...].T
    asked = got[K * B : K * B + K].astype(I32)
    onehot = jnp.concatenate(
        [jnp.where(sub == asked[r : r + 1, :], 1.0, 0.0).astype(BF16) for r in range(K)], axis=1
    )
    partial = partial + scatter(got, onehot)
    for n, dx in enumerate((0, 1, 3, 2)):
        halves[n].wait_recv()
        pick(dx, 1 - core)
    q0 = partial + forward(gt[...].T)

    w0 = blocks_times(p_v, q0)
    even, odd = pl.ds(0, N, stride=2), pl.ds(1, N, stride=2)
    s2[odd, :] = answers(w0, asked)
    c0_part = total(z0 * q0)
    out = to_owners([bucket(e) for e in spread(w0)])
    s2[even, :] = jnp.where(lane == 80, rho0_part, jnp.where(lane == 81, c0_part, out))
    exchange(2, s2, m2, rows=2)
    partial = blocks_times(d_v, w0)
    arrived(2, m2, rows=2)
    first = m2[even, :]
    sums = jnp.sum(first, axis=0, keepdims=True)
    lane1 = iota((1, N), 1)
    rho0, c0 = (total(jnp.where(lane1 == i, sums, 0.0)) for i in (80, 81))
    alpha = rho0 / c0
    image = partial + forward(m2[odd, :].T) + scatter(first.T, onehot)

    r1 = rhs - alpha * q0
    z1 = z0 - alpha * w0
    y1 = q0 - alpha * image
    rho1_part, c1_part, e1_part = total(r1 * z1), total(z1 * y1), total(z1 * q0)
    s3[...] = jnp.where(
        lane1 == 0, rho1_part, jnp.where(lane1 == 1, c1_part, jnp.where(lane1 == 2, e1_part, 0.0))
    )
    exchange(3, s3, m3, one=True)
    arrived(3, m3)
    sums = jnp.sum(m3[...], axis=0, keepdims=True)
    rho1, c1, e1 = (total(jnp.where(lane1 == i, sums, 0.0)) for i in range(3))
    beta = rho1 / rho0
    step = rho1 / (c1 + 2.0 * beta * e1 + beta * beta * c0)
    o_ref[0] = alpha * z0 + step * (z1 + beta * z0)
    o_ref[1] = r1 - step * (y1 + beta * q0)
    for n, dst, rows in ((0, m0, 1), (2, m2, 2), (3, m3, 1)):
        most = dst.at[0 : rows * (N - 1)]
        pltpu.make_async_copy(most, most, send.at[n]).wait()
    pltpu.make_async_copy(
        tiles.at[:, 0 : CHIPS - 1], tiles.at[:, 0 : CHIPS - 1], send.at[1]
    ).wait()
    for h in halves:
        h.wait_send()


def solve(right_side, diag_blocks, precond, upper_blocks, block_cols, slot_of_camera):
    shape = jax.ShapeDtypeStruct((B, N), F32)
    any_space = pl.BlockSpec(memory_space=pltpu.HBM)
    vmem = pl.BlockSpec(memory_space=pltpu.VMEM)
    row, two = pltpu.VMEM((N, N), F32), pltpu.VMEM((2 * N, N), F32)
    out = pl.pallas_call(
        kernel,
        out_shape=jax.ShapeDtypeStruct((2, B, N), F32),
        in_specs=[any_space] * 6,
        out_specs=vmem,
        scratch_shapes=[
            pltpu.VMEM((B, N), F32),
            pltpu.VMEM((B, B, N), F32),
            pltpu.VMEM((B, B, N), F32),
            pltpu.VMEM((B, B, K, N), F32),
            pltpu.VMEM((K, N), I32),
            pltpu.VMEM((N, N), I32),
            pltpu.SemaphoreType.DMA((6,)),
            row, row, pltpu.VMEM((B, N), F32), pltpu.VMEM((B, N, N), F32),
            two, two, pltpu.VMEM((1, N), F32), row,
            *[pltpu.SemaphoreType.DMA((4,))] * 5,
            pltpu.VMEM((N, N), F32),
            pltpu.VMEM((K * B, N), F32),
            pltpu.VMEM((N, N), I32),
            pltpu.VMEM((N, N), F32),
        ],
        compiler_params=pltpu.CompilerParams(collective_id=0, has_side_effects=True, vmem_limit_bytes=8 << 20),
    )(
        *[
            pltpu.with_memory_space_constraint(x, pltpu.HBM)
            for x in (
                right_side,
                diag_blocks,
                precond,
                jnp.transpose(upper_blocks, (1, 2, 0, 3)),
                block_cols,
                slot_of_camera.reshape(N, N),
            )
        ]
    )
    return out[0], out[1]


def solution(mesh):
    return jax.shard_map(
        solve,
        mesh=mesh,
        in_specs=(
            P(None, "rows"),
            P(None, None, "rows"),
            P(None, None, "rows"),
            P(None, None, None, "rows"),
            P(None, "rows"),
            P(),
        ),
        out_specs=(P(None, "rows"), P(None, "rows")),
        check_vma=False,
    )
```

```python
import functools
import itertools

import jax
import jax.numpy as jnp
from jax import lax
from jax.experimental import pallas as pl
from jax.experimental.pallas import tpu as pltpu
from jax.sharding import PartitionSpec as P

MESH = pl.DeviceIdType.MESH
B = 9
K = 8
N = 128
CHIPS = N // 2
PLANE = 16
F32, BF16, I32 = jnp.float32, jnp.bfloat16, jnp.int32


def hops(d):
    return sum(min(k, 4 - k) for k in d[:3])


STEPS = sorted(
    (d for d in itertools.product(range(4), range(4), range(4), range(2)) if any(d)),
    key=lambda d: -hops(d),
)


class Peers:
    def __init__(self, me):
        x, y, z, c = me // 32, lax.rem(me // 8, 4), lax.rem(me // 2, 4), lax.rem(me, 2)
        self.x = [lax.rem(x + d, 4) * 16 for d in range(4)]
        self.yz = [[lax.rem(y + i, 4) * 4 + lax.rem(z + j, 4) for j in range(4)] for i in range(4)]
        self.core = [c, 1 - c]
        self.half = [c * CHIPS, CHIPS - c * CHIPS]

    def chip(self, d):
        return self.x[d[0]] + self.yz[d[1]][d[2]]

    def device(self, d):
        return self.chip(d) * 2 + self.core[d[3]]

    def place(self, d):
        return self.chip(d) + self.half[d[3]]


def place_of(device):
    return lax.rem(device, 2) * CHIPS + device // 2


def iota(shape, dim):
    return lax.broadcasted_iota(I32, shape, dim)


def lanes(x, idx):
    return jnp.take_along_axis(x, idx, axis=1, mode="promise_in_bounds")


def rows8(row):
    return jnp.broadcast_to(row, (K, N))


def pieces(x):
    hi = x.astype(BF16)
    rest = x - hi.astype(F32)
    mid = rest.astype(BF16)
    return hi, mid, (rest - mid.astype(F32)).astype(BF16)


def total(x):
    rows = jnp.sum(x, axis=0, keepdims=True)
    return jnp.sum(rows, axis=1, keepdims=True)


def dot_t(a, b):
    return lax.dot_general(a, b, (((1,), (1,)), ((), ())), preferred_element_type=F32)


def blocks_times(m_ref, v):
    total = m_ref[0] * v[0:1]
    for a in range(1, B):
        total = total + m_ref[a] * v[a : a + 1]
    return total


def kernel(
    b_hbm, d_hbm, p_hbm, u_hbm, c_hbm, t_hbm, o_ref,
    b_v, d_v, p_v, u_v, c_v, t_v, in_sem,
    s0, m0, tile, tiles, s2, m2, s3, m3, send, recv, plane_recv, half_send, half_recv, pt, ft, wt, gt, wt2, po, tell_sem,
):
    me = lax.axis_index("rows")
    mine = place_of(me)
    core = lax.rem(me, 2)
    peers = Peers(me)
    barrier = pltpu.get_barrier_semaphore()

    def greet(steps):
        for d in steps:
            pl.semaphore_signal(
                barrier, inc=1, device_id=(peers.device(d),), device_id_type=MESH
            )

    far = [d for d in STEPS if hops(d) > 4]
    greet(far)
    copies = [
        pltpu.make_async_copy(src, dst, in_sem.at[i])
        for i, (src, dst) in enumerate(
            [(c_hbm, c_v), (t_hbm, t_v), (b_hbm, b_v), (p_hbm, p_v), (u_hbm, u_v), (d_hbm, d_v)]
        )
    ]
    for c in copies:
        c.start()
    greet(STEPS[len(far) :])

    def exchange(n, src, dst, rows=1, one=False):
        def of(ref, place):
            return ref.at[pl.ds(place * rows, rows)]

        for d in STEPS:
            pltpu.make_async_remote_copy(
                src_ref=src if one else of(src, peers.place(d)),
                dst_ref=of(dst, mine),
                send_sem=send.at[n],
                recv_sem=recv.at[n],
                device_id=(peers.device(d),),
                device_id_type=MESH,
            ).start()
        own = pl.ds(mine * rows, rows)
        dst[own, :] = src[...] if one else src[own, :]

    def arrived(n, dst, rows=1):
        most = dst.at[0 : rows * (N - 1)]
        pltpu.make_async_copy(most, most, recv.at[n]).wait()

    def plane(dx):
        return pl.multiple_of(lax.rem(me // 32 - dx + 4, 4) * PLANE, PLANE)

    copies[0].wait()
    copies[1].wait()
    cams = c_v[...]
    hi, lo = cams >> 7, cams & 127
    slots = jnp.zeros((K, N), I32)
    for r in range(N):
        slots = jnp.where(hi == r, lanes(rows8(t_v[r : r + 1, :]), lo), slots)
    device, offset = slots >> 7, slots & 127
    owner = (device & 1) * CHIPS + (device >> 1)

    sub = iota((N, N), 0)
    picks = [sub == owner[k : k + 1, :] for k in range(K)]
    ones = [jnp.where(p, 1.0, 0.0).astype(BF16) for p in picks]
    by_owner = jnp.concatenate(ones, axis=1)
    before = jnp.where(sub < iota((N, N), 1), 1.0, 0.0).astype(BF16)
    stacked = jnp.concatenate(ones, axis=0)
    earlier = jnp.dot(stacked, before, preferred_element_type=F32)
    counts = jnp.dot(stacked, jnp.ones((N, N), BF16), preferred_element_type=F32)
    base = jnp.zeros((N, N), F32)
    ranks = []
    for k in range(K):
        here = earlier[k * N : (k + 1) * N] + base
        ranks.append(jnp.sum(jnp.where(picks[k], here, 0.0), axis=0, keepdims=True))
        base = base + counts[k * N : (k + 1) * N]
    rank = jnp.concatenate(ranks, axis=0).astype(I32)
    sub8 = iota((K, N), 0)
    places = [rank[k : k + 1, :] == sub8 for k in range(K)]

    def spread(v):
        out = []
        for b in range(B):
            total = u_v[0, b] * v[0:1]
            for a in range(1, B):
                total = total + u_v[a, b] * v[a : a + 1]
            out.append(total)
        return out

    which = jnp.concatenate(
        [
            jnp.concatenate([jnp.where(p, float(k), 0.0) for k, p in enumerate(places)], axis=1),
            jnp.concatenate([jnp.where(p, iota((K, N), 1), 0).astype(F32) for p in places], axis=1),
        ],
        axis=0,
    )
    which = dot_t(which.astype(BF16), by_owner).astype(I32)
    list_at, slot_at = which[0:K], which[K : 2 * K]

    def bucket(e):
        out = lanes(rows8(e[0:1, :]), slot_at)
        for k in range(1, K):
            out = jnp.where(list_at == k, lanes(rows8(e[k : k + 1, :]), slot_at), out)
        return out

    def to_owners(lists):
        rest = jnp.zeros((N - K * len(lists), N), F32)
        return jnp.concatenate(lists + [rest] if rest.shape[0] else lists, axis=0).T

    def answers(v, asked):
        parts = [lanes(rows8(v[b : b + 1]), asked) for b in range(B)]
        return jnp.concatenate(parts + [jnp.zeros((N - K * B, N), F32)], axis=0).T

    def scatter(got, onehot):
        pt[...] = got
        flat = jnp.concatenate([pt[pl.ds(r, 16, stride=K), :] for r in range(K)], axis=1)
        out = dot_t(jnp.concatenate(pieces(flat), axis=0), onehot)
        return out[0:B] + out[16 : 16 + B] + out[32 : 32 + B]

    def forward(got):
        ft[...] = got[0 : K * B]
        total = [jnp.zeros((K, N), F32) for _ in range(B)]
        for b in range(B):
            g = jnp.zeros((K, N), F32)
            for r in range(K):
                row = rows8(ft[K * b + r : K * b + r + 1, :])
                g = jnp.where(rank == r, lanes(row, owner), g)
            for a in range(B):
                total[a] = total[a] + u_v[a, b] * g
        return jnp.concatenate([jnp.sum(t, axis=0, keepdims=True) for t in total], axis=0)

    copies[2].wait()
    copies[3].wait()
    rhs = b_v[...]
    z0 = blocks_times(p_v, rhs)
    tile[...] = z0
    copies[4].wait()
    copies[5].wait()
    bucket_offset = bucket(offset.astype(F32))
    s0[...] = to_owners([bucket(e) for e in spread(z0)] + [bucket_offset])
    wanted = to_owners([bucket_offset] * (N // K)).astype(I32)
    wt[...] = wanted
    pl.semaphore_wait(barrier, N - 1)

    tell = pltpu.make_async_remote_copy(
        src_ref=wt.at[pl.ds((1 - core) * CHIPS, CHIPS)],
        dst_ref=wt2,
        send_sem=tell_sem.at[0],
        recv_sem=tell_sem.at[1],
        device_id=(peers.device((0, 0, 0, 1)),),
        device_id_type=MESH,
    )
    tell.start()

    for dx in (2, 1, 3, 0):
        for d in STEPS:
            if d[0] == dx and d[3] == 0:
                pltpu.make_async_remote_copy(
                    src_ref=tile,
                    dst_ref=tiles.at[:, mine],
                    send_sem=send.at[1],
                    recv_sem=plane_recv.at[dx],
                    device_id=(peers.device(d),),
                    device_id_type=MESH,
                ).start()
    exchange(0, s0, m0)
    tiles[:, mine] = tile[...]

    lane = iota((N, N), 1)
    partial = blocks_times(d_v, z0)
    rho0_part = total(rhs * z0)
    block = iota((PLANE, N), 1) >> 3

    def pick(chips, index):
        here = pl.ds(core * CHIPS + chips, PLANE)
        out = jnp.zeros((PLANE, N), F32)
        for b in range(B):
            z = tiles[b, here, :]
            g = jnp.concatenate([lanes(z[i : i + K], index[i : i + K]) for i in (0, K)], axis=0)
            out = jnp.where(block == b, g, out)
        return out

    tell.wait_recv()
    halves = []
    for dx in (0, 1, 3, 2):
        n = PLANE - (dx == 0)
        pltpu.make_async_copy(tiles.at[:, 0:n], tiles.at[:, 0:n], plane_recv.at[dx]).wait()
        there = pl.ds(plane(dx), PLANE)
        po[there, :] = pick(plane(dx), wt2[there, :])
        halves.append(
            pltpu.make_async_remote_copy(
                src_ref=po.at[there],
                dst_ref=gt.at[pl.ds(core * CHIPS + plane(dx), PLANE)],
                send_sem=half_send.at[dx],
                recv_sem=half_recv.at[dx],
                device_id=(peers.device((0, 0, 0, 1)),),
                device_id_type=MESH,
            )
        )
        halves[-1].start()
    for dx in (0, 1, 3, 2):
        here = pl.ds(core * CHIPS + plane(dx), PLANE)
        gt[here, :] = pick(plane(dx), wt[here, :])
    arrived(0, m0)
    got = m0[...].T
    asked = got[K * B : K * B + K].astype(I32)
    onehot = jnp.concatenate(
        [jnp.where(sub == asked[r : r + 1, :], 1.0, 0.0).astype(BF16) for r in range(K)], axis=1
    )
    partial = partial + scatter(got, onehot)
    for h in halves:
        h.wait_recv()
    q0 = partial + forward(gt[...].T)

    w0 = blocks_times(p_v, q0)
    even, odd = pl.ds(0, N, stride=2), pl.ds(1, N, stride=2)
    s2[odd, :] = answers(w0, asked)
    c0_part = total(z0 * q0)
    out = to_owners([bucket(e) for e in spread(w0)])
    s2[even, :] = jnp.where(lane == 80, rho0_part, jnp.where(lane == 81, c0_part, out))
    exchange(2, s2, m2, rows=2)
    partial = blocks_times(d_v, w0)
    arrived(2, m2, rows=2)
    first = m2[even, :]
    sums = jnp.sum(first, axis=0, keepdims=True)
    lane1 = iota((1, N), 1)
    rho0, c0 = (total(jnp.where(lane1 == i, sums, 0.0)) for i in (80, 81))
    alpha = rho0 / c0
    image = partial + forward(m2[odd, :].T) + scatter(first.T, onehot)

    r1 = rhs - alpha * q0
    z1 = z0 - alpha * w0
    y1 = q0 - alpha * image
    rho1_part, c1_part, e1_part = total(r1 * z1), total(z1 * y1), total(z1 * q0)
    s3[...] = jnp.where(
        lane1 == 0, rho1_part, jnp.where(lane1 == 1, c1_part, jnp.where(lane1 == 2, e1_part, 0.0))
    )
    exchange(3, s3, m3, one=True)
    arrived(3, m3)
    sums = jnp.sum(m3[...], axis=0, keepdims=True)
    rho1, c1, e1 = (total(jnp.where(lane1 == i, sums, 0.0)) for i in range(3))
    beta = rho1 / rho0
    step = rho1 / (c1 + 2.0 * beta * e1 + beta * beta * c0)
    o_ref[0] = alpha * z0 + step * (z1 + beta * z0)
    o_ref[1] = r1 - step * (y1 + beta * q0)
    for n, dst, rows in ((0, m0, 1), (2, m2, 2), (3, m3, 1)):
        most = dst.at[0 : rows * (N - 1)]
        pltpu.make_async_copy(most, most, send.at[n]).wait()
    pltpu.make_async_copy(
        tiles.at[:, 0 : CHIPS - 1], tiles.at[:, 0 : CHIPS - 1], send.at[1]
    ).wait()
    for h in [tell] + halves:
        h.wait_send()


def solve(right_side, diag_blocks, precond, upper_blocks, block_cols, slot_of_camera):
    shape = jax.ShapeDtypeStruct((B, N), F32)
    any_space = pl.BlockSpec(memory_space=pltpu.HBM)
    vmem = pl.BlockSpec(memory_space=pltpu.VMEM)
    row, two = pltpu.VMEM((N, N), F32), pltpu.VMEM((2 * N, N), F32)
    out = pl.pallas_call(
        kernel,
        out_shape=jax.ShapeDtypeStruct((2, B, N), F32),
        in_specs=[any_space] * 6,
        out_specs=vmem,
        scratch_shapes=[
            pltpu.VMEM((B, N), F32),
            pltpu.VMEM((B, B, N), F32),
            pltpu.VMEM((B, B, N), F32),
            pltpu.VMEM((B, B, K, N), F32),
            pltpu.VMEM((K, N), I32),
            pltpu.VMEM((N, N), I32),
            pltpu.SemaphoreType.DMA((6,)),
            row, row, pltpu.VMEM((B, N), F32), pltpu.VMEM((B, N, N), F32),
            two, two, pltpu.VMEM((1, N), F32), row,
            *[pltpu.SemaphoreType.DMA((4,))] * 5,
            pltpu.VMEM((N, N), F32),
            pltpu.VMEM((K * B, N), F32),
            pltpu.VMEM((N, N), I32),
            pltpu.VMEM((N, N), F32),
            pltpu.VMEM((CHIPS, N), I32),
            pltpu.VMEM((CHIPS, N), F32),
            pltpu.SemaphoreType.DMA((2,)),
        ],
        compiler_params=pltpu.CompilerParams(collective_id=0, has_side_effects=True, vmem_limit_bytes=8 << 20),
    )(
        *[
            pltpu.with_memory_space_constraint(x, pltpu.HBM)
            for x in (
                right_side,
                diag_blocks,
                precond,
                jnp.transpose(upper_blocks, (1, 2, 0, 3)),
                block_cols,
                slot_of_camera.reshape(N, N),
            )
        ]
    )
    return out[0], out[1]


def solution(mesh):
    return jax.shard_map(
        solve,
        mesh=mesh,
        in_specs=(
            P(None, "rows"),
            P(None, None, "rows"),
            P(None, None, "rows"),
            P(None, None, None, "rows"),
            P(None, "rows"),
            P(),
        ),
        out_specs=(P(None, "rows"), P(None, "rows")),
        check_vma=False,
    )
```

```python
import functools
import itertools

import jax
import jax.numpy as jnp
from jax import lax
from jax.experimental import pallas as pl
from jax.experimental.pallas import tpu as pltpu
from jax.sharding import PartitionSpec as P

MESH = pl.DeviceIdType.MESH
B = 9
K = 8
N = 128
CHIPS = N // 2
PLANE = 16
F32, BF16, I32 = jnp.float32, jnp.bfloat16, jnp.int32


def hops(d):
    return sum(min(k, 4 - k) for k in d[:3])


STEPS = sorted(
    (d for d in itertools.product(range(4), range(4), range(4), range(2)) if any(d)),
    key=lambda d: -hops(d),
)


class Peers:
    def __init__(self, me):
        x, y, z, c = me >> 5, (me >> 3) & 3, (me >> 1) & 3, me & 1
        self.x = [((x + d) & 3) * 16 for d in range(4)]
        self.yz = [[((y + i) & 3) * 4 + ((z + j) & 3) for j in range(4)] for i in range(4)]
        self.core = [c, 1 - c]
        self.half = [c * CHIPS, CHIPS - c * CHIPS]

    def chip(self, d):
        return self.x[d[0]] + self.yz[d[1]][d[2]]

    def device(self, d):
        return self.chip(d) * 2 + self.core[d[3]]

    def place(self, d):
        return self.chip(d) + self.half[d[3]]


def place_of(device):
    return lax.rem(device, 2) * CHIPS + device // 2


def iota(shape, dim):
    return lax.broadcasted_iota(I32, shape, dim)


def lanes(x, idx):
    return jnp.take_along_axis(x, idx, axis=1, mode="promise_in_bounds")


def rows8(row):
    return jnp.broadcast_to(row, (K, N))


def pieces(x):
    hi = x.astype(BF16)
    rest = x - hi.astype(F32)
    mid = rest.astype(BF16)
    return hi, mid, (rest - mid.astype(F32)).astype(BF16)


def total(x):
    rows = jnp.sum(x, axis=0, keepdims=True)
    return jnp.sum(rows, axis=1, keepdims=True)


def dot_t(a, b):
    return lax.dot_general(a, b, (((1,), (1,)), ((), ())), preferred_element_type=F32)


def blocks_times(m_ref, v):
    total = m_ref[0] * v[0:1]
    for a in range(1, B):
        total = total + m_ref[a] * v[a : a + 1]
    return total


def kernel(
    b_hbm, d_hbm, p_hbm, u_hbm, c_hbm, t_hbm, o_ref,
    b_v, d_v, p_v, u_v, c_v, t_v, in_sem,
    s0, m0, tile, tiles, s2, m2, s3, m3, send, recv, plane_recv, half_send, half_recv, pt, ft, wt, gt, wt2, po, tell_sem,
):
    me = lax.axis_index("rows")
    mine = place_of(me)
    core = lax.rem(me, 2)
    peers = Peers(me)
    barrier = pltpu.get_barrier_semaphore()

    def greet(steps):
        for d in steps:
            pl.semaphore_signal(
                barrier, inc=1, device_id=(peers.device(d),), device_id_type=MESH
            )

    far = [d for d in STEPS if hops(d) > 4]
    greet(far)
    copies = [
        pltpu.make_async_copy(src, dst, in_sem.at[i])
        for i, (src, dst) in enumerate(
            [(c_hbm, c_v), (t_hbm, t_v), (b_hbm, b_v), (p_hbm, p_v), (u_hbm, u_v), (d_hbm, d_v)]
        )
    ]
    for c in copies:
        c.start()
    greet(STEPS[len(far) :])

    def exchange(n, src, dst, rows=1, one=False):
        def of(ref, place):
            return ref.at[pl.ds(place * rows, rows)]

        for d in STEPS:
            pltpu.make_async_remote_copy(
                src_ref=src if one else of(src, peers.place(d)),
                dst_ref=of(dst, mine),
                send_sem=send.at[n],
                recv_sem=recv.at[n],
                device_id=(peers.device(d),),
                device_id_type=MESH,
            ).start()
        own = pl.ds(mine * rows, rows)
        dst[own, :] = src[...] if one else src[own, :]

    def arrived(n, dst, rows=1):
        most = dst.at[0 : rows * (N - 1)]
        pltpu.make_async_copy(most, most, recv.at[n]).wait()

    def plane(dx):
        return pl.multiple_of(lax.rem(me // 32 - dx + 4, 4) * PLANE, PLANE)

    copies[0].wait()
    copies[1].wait()
    cams = c_v[...]
    hi, lo = cams >> 7, cams & 127
    slots = jnp.zeros((K, N), I32)
    for r in range(N):
        slots = jnp.where(hi == r, lanes(rows8(t_v[r : r + 1, :]), lo), slots)
    device, offset = slots >> 7, slots & 127
    owner = (device & 1) * CHIPS + (device >> 1)

    sub = iota((N, N), 0)
    picks = [sub == owner[k : k + 1, :] for k in range(K)]
    ones = [jnp.where(p, 1.0, 0.0).astype(BF16) for p in picks]
    by_owner = jnp.concatenate(ones, axis=1)
    before = jnp.where(sub < iota((N, N), 1), 1.0, 0.0).astype(BF16)
    stacked = jnp.concatenate(ones, axis=0)
    earlier = jnp.dot(stacked, before, preferred_element_type=F32)
    counts = jnp.dot(stacked, jnp.ones((N, N), BF16), preferred_element_type=F32)
    base = jnp.zeros((N, N), F32)
    ranks = []
    for k in range(K):
        here = earlier[k * N : (k + 1) * N] + base
        ranks.append(jnp.sum(jnp.where(picks[k], here, 0.0), axis=0, keepdims=True))
        base = base + counts[k * N : (k + 1) * N]
    rank = jnp.concatenate(ranks, axis=0).astype(I32)
    sub8 = iota((K, N), 0)
    places = [rank[k : k + 1, :] == sub8 for k in range(K)]

    def spread(v):
        out = []
        for b in range(B):
            total = u_v[0, b] * v[0:1]
            for a in range(1, B):
                total = total + u_v[a, b] * v[a : a + 1]
            out.append(total)
        return out

    which = jnp.concatenate(
        [
            jnp.concatenate([jnp.where(p, float(k), 0.0) for k, p in enumerate(places)], axis=1),
            jnp.concatenate([jnp.where(p, iota((K, N), 1), 0).astype(F32) for p in places], axis=1),
        ],
        axis=0,
    )
    which = dot_t(which.astype(BF16), by_owner).astype(I32)
    list_at, slot_at = which[0:K], which[K : 2 * K]

    def bucket(e):
        out = lanes(rows8(e[0:1, :]), slot_at)
        for k in range(1, K):
            out = jnp.where(list_at == k, lanes(rows8(e[k : k + 1, :]), slot_at), out)
        return out

    def to_owners(lists):
        rest = jnp.zeros((N - K * len(lists), N), F32)
        return jnp.concatenate(lists + [rest] if rest.shape[0] else lists, axis=0).T

    def answers(v, asked):
        parts = [lanes(rows8(v[b : b + 1]), asked) for b in range(B)]
        return jnp.concatenate(parts + [jnp.zeros((N - K * B, N), F32)], axis=0).T

    def scatter(got, onehot):
        pt[...] = got
        flat = jnp.concatenate([pt[pl.ds(r, 16, stride=K), :] for r in range(K)], axis=1)
        out = dot_t(jnp.concatenate(pieces(flat), axis=0), onehot)
        return out[0:B] + out[16 : 16 + B] + out[32 : 32 + B]

    def forward(got):
        ft[...] = got[0 : K * B]
        total = [jnp.zeros((K, N), F32) for _ in range(B)]
        for b in range(B):
            g = jnp.zeros((K, N), F32)
            for r in range(K):
                row = rows8(ft[K * b + r : K * b + r + 1, :])
                g = jnp.where(rank == r, lanes(row, owner), g)
            for a in range(B):
                total[a] = total[a] + u_v[a, b] * g
        return jnp.concatenate([jnp.sum(t, axis=0, keepdims=True) for t in total], axis=0)

    copies[2].wait()
    copies[3].wait()
    rhs = b_v[...]
    z0 = blocks_times(p_v, rhs)
    tile[...] = z0
    copies[4].wait()
    copies[5].wait()
    bucket_offset = bucket(offset.astype(F32))
    s0[...] = to_owners([bucket(e) for e in spread(z0)] + [bucket_offset])
    wanted = to_owners([bucket_offset] * (N // K)).astype(I32)
    wt[...] = wanted
    pl.semaphore_wait(barrier, N - 1)

    tell = pltpu.make_async_remote_copy(
        src_ref=wt.at[pl.ds((1 - core) * CHIPS, CHIPS)],
        dst_ref=wt2,
        send_sem=tell_sem.at[0],
        recv_sem=tell_sem.at[1],
        device_id=(peers.device((0, 0, 0, 1)),),
        device_id_type=MESH,
    )
    tell.start()

    for dx in (2, 1, 3, 0):
        for d in STEPS:
            if d[0] == dx and d[3] == 0:
                pltpu.make_async_remote_copy(
                    src_ref=tile,
                    dst_ref=tiles.at[:, mine],
                    send_sem=send.at[1],
                    recv_sem=plane_recv.at[dx],
                    device_id=(peers.device(d),),
                    device_id_type=MESH,
                ).start()
    exchange(0, s0, m0)
    tiles[:, mine] = tile[...]

    lane = iota((N, N), 1)
    partial = blocks_times(d_v, z0)
    rho0_part = total(rhs * z0)
    block = iota((PLANE, N), 1) >> 3

    def pick(chips, index):
        here = pl.ds(core * CHIPS + chips, PLANE)
        out = jnp.zeros((PLANE, N), F32)
        for b in range(B):
            z = tiles[b, here, :]
            g = jnp.concatenate([lanes(z[i : i + K], index[i : i + K]) for i in (0, K)], axis=0)
            out = jnp.where(block == b, g, out)
        return out

    tell.wait_recv()
    halves = []
    for dx in (0, 1, 3, 2):
        n = PLANE - (dx == 0)
        pltpu.make_async_copy(tiles.at[:, 0:n], tiles.at[:, 0:n], plane_recv.at[dx]).wait()
        there = pl.ds(plane(dx), PLANE)
        po[there, :] = pick(plane(dx), wt2[there, :])
        halves.append(
            pltpu.make_async_remote_copy(
                src_ref=po.at[there],
                dst_ref=gt.at[pl.ds(core * CHIPS + plane(dx), PLANE)],
                send_sem=half_send.at[dx],
                recv_sem=half_recv.at[dx],
                device_id=(peers.device((0, 0, 0, 1)),),
                device_id_type=MESH,
            )
        )
        halves[-1].start()
    for dx in (0, 1, 3, 2):
        here = pl.ds(core * CHIPS + plane(dx), PLANE)
        gt[here, :] = pick(plane(dx), wt[here, :])
    arrived(0, m0)
    got = m0[...].T
    asked = got[K * B : K * B + K].astype(I32)
    onehot = jnp.concatenate(
        [jnp.where(sub == asked[r : r + 1, :], 1.0, 0.0).astype(BF16) for r in range(K)], axis=1
    )
    partial = partial + scatter(got, onehot)
    for h in halves:
        h.wait_recv()
    q0 = partial + forward(gt[...].T)

    w0 = blocks_times(p_v, q0)
    even, odd = pl.ds(0, N, stride=2), pl.ds(1, N, stride=2)
    s2[odd, :] = answers(w0, asked)
    c0_part = total(z0 * q0)
    out = to_owners([bucket(e) for e in spread(w0)])
    s2[even, :] = jnp.where(lane == 80, rho0_part, jnp.where(lane == 81, c0_part, out))
    exchange(2, s2, m2, rows=2)
    partial = blocks_times(d_v, w0)
    arrived(2, m2, rows=2)
    first = m2[even, :]
    sums = jnp.sum(first, axis=0, keepdims=True)
    lane1 = iota((1, N), 1)
    rho0, c0 = (total(jnp.where(lane1 == i, sums, 0.0)) for i in (80, 81))
    alpha = rho0 / c0
    image = partial + forward(m2[odd, :].T) + scatter(first.T, onehot)

    r1 = rhs - alpha * q0
    z1 = z0 - alpha * w0
    y1 = q0 - alpha * image
    rho1_part, c1_part, e1_part = total(r1 * z1), total(z1 * y1), total(z1 * q0)
    s3[...] = jnp.where(
        lane1 == 0, rho1_part, jnp.where(lane1 == 1, c1_part, jnp.where(lane1 == 2, e1_part, 0.0))
    )
    exchange(3, s3, m3, one=True)
    for n, dst, rows in ((0, m0, 1), (2, m2, 2)):
        most = dst.at[0 : rows * (N - 1)]
        pltpu.make_async_copy(most, most, send.at[n]).wait()
    pltpu.make_async_copy(
        tiles.at[:, 0 : CHIPS - 1], tiles.at[:, 0 : CHIPS - 1], send.at[1]
    ).wait()
    for h in [tell] + halves:
        h.wait_send()
    arrived(3, m3)
    sums = jnp.sum(m3[...], axis=0, keepdims=True)
    rho1, c1, e1 = (total(jnp.where(lane1 == i, sums, 0.0)) for i in range(3))
    beta = rho1 / rho0
    step = rho1 / (c1 + 2.0 * beta * e1 + beta * beta * c0)
    o_ref[0] = alpha * z0 + step * (z1 + beta * z0)
    o_ref[1] = r1 - step * (y1 + beta * q0)
    most = m3.at[0 : N - 1]
    pltpu.make_async_copy(most, most, send.at[3]).wait()


def solve(right_side, diag_blocks, precond, upper_blocks, block_cols, slot_of_camera):
    shape = jax.ShapeDtypeStruct((B, N), F32)
    any_space = pl.BlockSpec(memory_space=pltpu.HBM)
    vmem = pl.BlockSpec(memory_space=pltpu.VMEM)
    row, two = pltpu.VMEM((N, N), F32), pltpu.VMEM((2 * N, N), F32)
    out = pl.pallas_call(
        kernel,
        out_shape=jax.ShapeDtypeStruct((2, B, N), F32),
        in_specs=[any_space] * 6,
        out_specs=vmem,
        scratch_shapes=[
            pltpu.VMEM((B, N), F32),
            pltpu.VMEM((B, B, N), F32),
            pltpu.VMEM((B, B, N), F32),
            pltpu.VMEM((B, B, K, N), F32),
            pltpu.VMEM((K, N), I32),
            pltpu.VMEM((N, N), I32),
            pltpu.SemaphoreType.DMA((6,)),
            row, row, pltpu.VMEM((B, N), F32), pltpu.VMEM((B, N, N), F32),
            two, two, pltpu.VMEM((1, N), F32), row,
            *[pltpu.SemaphoreType.DMA((4,))] * 5,
            pltpu.VMEM((N, N), F32),
            pltpu.VMEM((K * B, N), F32),
            pltpu.VMEM((N, N), I32),
            pltpu.VMEM((N, N), F32),
            pltpu.VMEM((CHIPS, N), I32),
            pltpu.VMEM((CHIPS, N), F32),
            pltpu.SemaphoreType.DMA((2,)),
        ],
        compiler_params=pltpu.CompilerParams(collective_id=0, has_side_effects=True, vmem_limit_bytes=8 << 20),
    )(
        *[
            pltpu.with_memory_space_constraint(x, pltpu.HBM)
            for x in (
                right_side,
                diag_blocks,
                precond,
                jnp.transpose(upper_blocks, (1, 2, 0, 3)),
                block_cols,
                slot_of_camera.reshape(N, N),
            )
        ]
    )
    return out[0], out[1]


def solution(mesh):
    return jax.shard_map(
        solve,
        mesh=mesh,
        in_specs=(
            P(None, "rows"),
            P(None, None, "rows"),
            P(None, None, "rows"),
            P(None, None, None, "rows"),
            P(None, "rows"),
            P(),
        ),
        out_specs=(P(None, "rows"), P(None, "rows")),
        check_vma=False,
    )
```

```python
import functools
import itertools

import jax
import jax.numpy as jnp
from jax import lax
from jax.experimental import pallas as pl
from jax.experimental.pallas import tpu as pltpu
from jax.sharding import PartitionSpec as P

MESH = pl.DeviceIdType.MESH
B = 9
K = 8
N = 128
CHIPS = N // 2
PLANE = 16
F32, BF16, I32 = jnp.float32, jnp.bfloat16, jnp.int32


def hops(d):
    return sum(min(k, 4 - k) for k in d[:3])


STEPS = sorted(
    (d for d in itertools.product(range(4), range(4), range(4), range(2)) if any(d)),
    key=lambda d: -hops(d),
)


class Peers:
    def __init__(self, me):
        x, y, z, c = me // 32, lax.rem(me // 8, 4), lax.rem(me // 2, 4), lax.rem(me, 2)
        self.x = [lax.rem(x + d, 4) * 16 for d in range(4)]
        self.yz = [[lax.rem(y + i, 4) * 4 + lax.rem(z + j, 4) for j in range(4)] for i in range(4)]
        self.core = [c, 1 - c]
        self.half = [c * CHIPS, CHIPS - c * CHIPS]

    def chip(self, d):
        return self.x[d[0]] + self.yz[d[1]][d[2]]

    def device(self, d):
        return self.chip(d) * 2 + self.core[d[3]]

    def place(self, d):
        return self.chip(d) + self.half[d[3]]


def place_of(device):
    return lax.rem(device, 2) * CHIPS + device // 2


def iota(shape, dim):
    return lax.broadcasted_iota(I32, shape, dim)


def lanes(x, idx):
    return jnp.take_along_axis(x, idx, axis=1, mode="promise_in_bounds")


def rows8(row):
    return jnp.broadcast_to(row, (K, N))


def pieces(x):
    hi = x.astype(BF16)
    rest = x - hi.astype(F32)
    mid = rest.astype(BF16)
    return hi, mid, (rest - mid.astype(F32)).astype(BF16)


def total(x):
    rows = jnp.sum(x, axis=0, keepdims=True)
    return jnp.sum(rows, axis=1, keepdims=True)


def dot_t(a, b):
    return lax.dot_general(a, b, (((1,), (1,)), ((), ())), preferred_element_type=F32)


def blocks_times(m_ref, v):
    total = m_ref[0] * v[0:1]
    for a in range(1, B):
        total = total + m_ref[a] * v[a : a + 1]
    return total


def kernel(
    b_hbm, d_hbm, p_hbm, u_hbm, c_hbm, t_hbm, o_ref,
    b_v, d_v, p_v, u_v, c_v, t_v, in_sem,
    s0, m0, tile, tiles, s2, m2, s3, m3, send, recv, plane_recv, half_send, half_recv, pt, ft, wt, gt, wt2, po, tell_sem,
):
    me = lax.axis_index("rows")
    mine = place_of(me)
    core = lax.rem(me, 2)
    peers = Peers(me)
    barrier = pltpu.get_barrier_semaphore()

    def greet(steps):
        for d in steps:
            pl.semaphore_signal(
                barrier, inc=1, device_id=(peers.device(d),), device_id_type=MESH
            )

    far = [d for d in STEPS if hops(d) > 4]
    greet(far)
    copies = [
        pltpu.make_async_copy(src, dst, in_sem.at[i])
        for i, (src, dst) in enumerate(
            [(c_hbm, c_v), (t_hbm, t_v), (b_hbm, b_v), (p_hbm, p_v), (u_hbm, u_v), (d_hbm, d_v)]
        )
    ]
    for c in copies:
        c.start()
    greet(STEPS[len(far) :])

    def exchange(n, src, dst, rows=1, one=False):
        def of(ref, place):
            return ref.at[pl.ds(place * rows, rows)]

        for d in STEPS:
            pltpu.make_async_remote_copy(
                src_ref=src if one else of(src, peers.place(d)),
                dst_ref=of(dst, mine),
                send_sem=send.at[n],
                recv_sem=recv.at[n],
                device_id=(peers.device(d),),
                device_id_type=MESH,
            ).start()
        own = pl.ds(mine * rows, rows)
        dst[own, :] = src[...] if one else src[own, :]

    def arrived(n, dst, rows=1):
        most = dst.at[0 : rows * (N - 1)]
        pltpu.make_async_copy(most, most, recv.at[n]).wait()

    def plane(dx):
        return pl.multiple_of(lax.rem(me // 32 - dx + 4, 4) * PLANE, PLANE)

    copies[0].wait()
    copies[1].wait()
    cams = c_v[...]
    hi, lo = cams >> 7, cams & 127
    slots = jnp.zeros((K, N), I32)
    for r in range(N):
        slots = jnp.where(hi == r, lanes(rows8(t_v[r : r + 1, :]), lo), slots)
    device, offset = slots >> 7, slots & 127
    owner = (device & 1) * CHIPS + (device >> 1)

    sub = iota((N, N), 0)
    picks = [sub == owner[k : k + 1, :] for k in range(K)]
    ones = [jnp.where(p, 1.0, 0.0).astype(BF16) for p in picks]
    by_owner = jnp.concatenate(ones, axis=1)
    before = jnp.where(sub < iota((N, N), 1), 1.0, 0.0).astype(BF16)
    stacked = jnp.concatenate(ones, axis=0)
    earlier = jnp.dot(stacked, before, preferred_element_type=F32)
    counts = jnp.dot(stacked, jnp.ones((N, N), BF16), preferred_element_type=F32)
    base = jnp.zeros((N, N), F32)
    ranks = []
    for k in range(K):
        here = earlier[k * N : (k + 1) * N] + base
        ranks.append(jnp.sum(jnp.where(picks[k], here, 0.0), axis=0, keepdims=True))
        base = base + counts[k * N : (k + 1) * N]
    rank = jnp.concatenate(ranks, axis=0).astype(I32)
    sub8 = iota((K, N), 0)
    places = [rank[k : k + 1, :] == sub8 for k in range(K)]

    def spread(v):
        out = []
        for b in range(B):
            total = u_v[0, b] * v[0:1]
            for a in range(1, B):
                total = total + u_v[a, b] * v[a : a + 1]
            out.append(total)
        return out

    which = jnp.concatenate(
        [
            jnp.concatenate([jnp.where(p, float(k), 0.0) for k, p in enumerate(places)], axis=1),
            jnp.concatenate([jnp.where(p, iota((K, N), 1), 0).astype(F32) for p in places], axis=1),
        ],
        axis=0,
    )
    which = dot_t(which.astype(BF16), by_owner).astype(I32)
    list_at, slot_at = which[0:K], which[K : 2 * K]

    def bucket(e):
        out = lanes(rows8(e[0:1, :]), slot_at)
        for k in range(1, K):
            out = jnp.where(list_at == k, lanes(rows8(e[k : k + 1, :]), slot_at), out)
        return out

    def to_owners(lists):
        rest = jnp.zeros((N - K * len(lists), N), F32)
        return jnp.concatenate(lists + [rest] if rest.shape[0] else lists, axis=0).T

    def answers(v, asked):
        parts = [lanes(rows8(v[b : b + 1]), asked) for b in range(B)]
        return jnp.concatenate(parts + [jnp.zeros((N - K * B, N), F32)], axis=0).T

    def scatter(got, onehot):
        pt[...] = got
        flat = jnp.concatenate([pt[pl.ds(r, 16, stride=K), :] for r in range(K)], axis=1)
        out = dot_t(jnp.concatenate(pieces(flat), axis=0), onehot)
        return out[0:B] + out[16 : 16 + B] + out[32 : 32 + B]

    def forward(got):
        ft[...] = got[0 : K * B]
        total = [jnp.zeros((K, N), F32) for _ in range(B)]
        for b in range(B):
            g = jnp.zeros((K, N), F32)
            for r in range(K):
                row = rows8(ft[K * b + r : K * b + r + 1, :])
                g = jnp.where(rank == r, lanes(row, owner), g)
            for a in range(B):
                total[a] = total[a] + u_v[a, b] * g
        return jnp.concatenate([jnp.sum(t, axis=0, keepdims=True) for t in total], axis=0)

    copies[2].wait()
    copies[3].wait()
    rhs = b_v[...]
    z0 = blocks_times(p_v, rhs)
    tile[...] = z0
    pl.semaphore_wait(barrier, N - 1)
    for dx in (2, 1, 3, 0):
        for d in STEPS:
            if d[0] == dx and d[3] == 0:
                pltpu.make_async_remote_copy(
                    src_ref=tile,
                    dst_ref=tiles.at[:, mine],
                    send_sem=send.at[1],
                    recv_sem=plane_recv.at[dx],
                    device_id=(peers.device(d),),
                    device_id_type=MESH,
                ).start()
    copies[4].wait()
    copies[5].wait()
    bucket_offset = bucket(offset.astype(F32))
    s0[...] = to_owners([bucket(e) for e in spread(z0)] + [bucket_offset])
    wanted = to_owners([bucket_offset] * (N // K)).astype(I32)
    wt[...] = wanted

    tell = pltpu.make_async_remote_copy(
        src_ref=wt.at[pl.ds((1 - core) * CHIPS, CHIPS)],
        dst_ref=wt2,
        send_sem=tell_sem.at[0],
        recv_sem=tell_sem.at[1],
        device_id=(peers.device((0, 0, 0, 1)),),
        device_id_type=MESH,
    )
    tell.start()

    exchange(0, s0, m0)
    tiles[:, mine] = tile[...]

    lane = iota((N, N), 1)
    partial = blocks_times(d_v, z0)
    rho0_part = total(rhs * z0)
    block = iota((PLANE, N), 1) >> 3

    def pick(chips, index):
        here = pl.ds(core * CHIPS + chips, PLANE)
        out = jnp.zeros((PLANE, N), F32)
        for b in range(B):
            z = tiles[b, here, :]
            g = jnp.concatenate([lanes(z[i : i + K], index[i : i + K]) for i in (0, K)], axis=0)
            out = jnp.where(block == b, g, out)
        return out

    tell.wait_recv()
    halves = []
    for dx in (0, 1, 3, 2):
        n = PLANE - (dx == 0)
        pltpu.make_async_copy(tiles.at[:, 0:n], tiles.at[:, 0:n], plane_recv.at[dx]).wait()
        there = pl.ds(plane(dx), PLANE)
        po[there, :] = pick(plane(dx), wt2[there, :])
        halves.append(
            pltpu.make_async_remote_copy(
                src_ref=po.at[there],
                dst_ref=gt.at[pl.ds(core * CHIPS + plane(dx), PLANE)],
                send_sem=half_send.at[dx],
                recv_sem=half_recv.at[dx],
                device_id=(peers.device((0, 0, 0, 1)),),
                device_id_type=MESH,
            )
        )
        halves[-1].start()
    for dx in (0, 1, 3, 2):
        here = pl.ds(core * CHIPS + plane(dx), PLANE)
        gt[here, :] = pick(plane(dx), wt[here, :])
    arrived(0, m0)
    got = m0[...].T
    asked = got[K * B : K * B + K].astype(I32)
    onehot = jnp.concatenate(
        [jnp.where(sub == asked[r : r + 1, :], 1.0, 0.0).astype(BF16) for r in range(K)], axis=1
    )
    partial = partial + scatter(got, onehot)
    for h in halves:
        h.wait_recv()
    q0 = partial + forward(gt[...].T)

    w0 = blocks_times(p_v, q0)
    even, odd = pl.ds(0, N, stride=2), pl.ds(1, N, stride=2)
    s2[odd, :] = answers(w0, asked)
    c0_part = total(z0 * q0)
    out = to_owners([bucket(e) for e in spread(w0)])
    s2[even, :] = jnp.where(lane == 80, rho0_part, jnp.where(lane == 81, c0_part, out))
    exchange(2, s2, m2, rows=2)
    partial = blocks_times(d_v, w0)
    arrived(2, m2, rows=2)
    first = m2[even, :]
    sums = jnp.sum(first, axis=0, keepdims=True)
    lane1 = iota((1, N), 1)
    rho0, c0 = (total(jnp.where(lane1 == i, sums, 0.0)) for i in (80, 81))
    alpha = rho0 / c0
    image = partial + forward(m2[odd, :].T) + scatter(first.T, onehot)

    r1 = rhs - alpha * q0
    z1 = z0 - alpha * w0
    y1 = q0 - alpha * image
    rho1_part, c1_part, e1_part = total(r1 * z1), total(z1 * y1), total(z1 * q0)
    s3[...] = jnp.where(
        lane1 == 0, rho1_part, jnp.where(lane1 == 1, c1_part, jnp.where(lane1 == 2, e1_part, 0.0))
    )
    exchange(3, s3, m3, one=True)
    arrived(3, m3)
    sums = jnp.sum(m3[...], axis=0, keepdims=True)
    rho1, c1, e1 = (total(jnp.where(lane1 == i, sums, 0.0)) for i in range(3))
    beta = rho1 / rho0
    step = rho1 / (c1 + 2.0 * beta * e1 + beta * beta * c0)
    o_ref[0] = alpha * z0 + step * (z1 + beta * z0)
    o_ref[1] = r1 - step * (y1 + beta * q0)
    for n, dst, rows in ((0, m0, 1), (2, m2, 2), (3, m3, 1)):
        most = dst.at[0 : rows * (N - 1)]
        pltpu.make_async_copy(most, most, send.at[n]).wait()
    pltpu.make_async_copy(
        tiles.at[:, 0 : CHIPS - 1], tiles.at[:, 0 : CHIPS - 1], send.at[1]
    ).wait()
    for h in [tell] + halves:
        h.wait_send()


def solve(right_side, diag_blocks, precond, upper_blocks, block_cols, slot_of_camera):
    shape = jax.ShapeDtypeStruct((B, N), F32)
    any_space = pl.BlockSpec(memory_space=pltpu.HBM)
    vmem = pl.BlockSpec(memory_space=pltpu.VMEM)
    row, two = pltpu.VMEM((N, N), F32), pltpu.VMEM((2 * N, N), F32)
    out = pl.pallas_call(
        kernel,
        out_shape=jax.ShapeDtypeStruct((2, B, N), F32),
        in_specs=[any_space] * 6,
        out_specs=vmem,
        scratch_shapes=[
            pltpu.VMEM((B, N), F32),
            pltpu.VMEM((B, B, N), F32),
            pltpu.VMEM((B, B, N), F32),
            pltpu.VMEM((B, B, K, N), F32),
            pltpu.VMEM((K, N), I32),
            pltpu.VMEM((N, N), I32),
            pltpu.SemaphoreType.DMA((6,)),
            row, row, pltpu.VMEM((B, N), F32), pltpu.VMEM((B, N, N), F32),
            two, two, pltpu.VMEM((1, N), F32), row,
            *[pltpu.SemaphoreType.DMA((4,))] * 5,
            pltpu.VMEM((N, N), F32),
            pltpu.VMEM((K * B, N), F32),
            pltpu.VMEM((N, N), I32),
            pltpu.VMEM((N, N), F32),
            pltpu.VMEM((CHIPS, N), I32),
            pltpu.VMEM((CHIPS, N), F32),
            pltpu.SemaphoreType.DMA((2,)),
        ],
        compiler_params=pltpu.CompilerParams(collective_id=0, has_side_effects=True, vmem_limit_bytes=8 << 20),
    )(
        *[
            pltpu.with_memory_space_constraint(x, pltpu.HBM)
            for x in (
                right_side,
                diag_blocks,
                precond,
                jnp.transpose(upper_blocks, (1, 2, 0, 3)),
                block_cols,
                slot_of_camera.reshape(N, N),
            )
        ]
    )
    return out[0], out[1]


def solution(mesh):
    return jax.shard_map(
        solve,
        mesh=mesh,
        in_specs=(
            P(None, "rows"),
            P(None, None, "rows"),
            P(None, None, "rows"),
            P(None, None, None, "rows"),
            P(None, "rows"),
            P(),
        ),
        out_specs=(P(None, "rows"), P(None, "rows")),
        check_vma=False,
    )
```
